32 devices in a mesh: gx: 4 (over y, x), gy: 8 (over z, core).
Axes of the slice: x: 2, y: 2, z: 4, core: 2. Of those that a mesh axis runs over, the one named last changes fastest.
Arguments:
- thermal_field: float32 [192, 192, 128], P('gx', 'gy'), may hold values from -6 to 6
- generator_keys: int32 [6], replicated, may hold values from 0 to 1048575
- slab_top_offset: int32 [1], replicated, may hold values from 0 to 2047
Outputs:
- factor_x: float32 [192, 64], P('gx')
- factor_y: float32 [192, 64], P('gy')
- factor_z: float32 [128, 64], replicated
- core: float32 [128, 128, 128], P('gx', 'gy')
The draws below stay inside these ranges and needn't reach their ends.
All inputs are finite; a program needn't handle non-finite values.
Results may differ from the reference program's by a relative error of at most 0.000071.
Values sent between devices are 32-bit elements; how exact they have to be, the bound alone decides.
A program may use at most 64 MiB of HBM per device.

```python
import math
import jax
import jax.numpy as jnp
from jax import lax

VERTICAL_COUNT = 128
RANK = 64
TARGET_RANK = 128
ZONAL_COUNT = 192
MERIDIONAL_COUNT = 192


def place_ends(entries, key, smallest, top_value):
    index_at = [jax.random.randint(jax.random.fold_in(key, axis), (), 0, length) for axis, length in enumerate(entries.shape)]
    widest = entries.shape.index(max(entries.shape))
    beside = index_at[:widest] + [(index_at[widest] + 1) % entries.shape[widest]] + index_at[widest + 1:]
    return entries.at[tuple(index_at)].set(smallest).at[tuple(beside)].set(top_value)


def levels(stream_key, shape, cuts, low, largest):
    def one(axis_at, parts):
        draws = jax.random.uniform(jax.random.fold_in(jax.random.fold_in(stream_key, 6), axis_at), (parts,), jnp.float32, low / len(cuts), largest / len(cuts))
        return jnp.repeat(jnp.exp(draws), shape[axis_at] // parts).reshape((-1,) + (1,) * (len(shape) - axis_at - 1))

    level = one(*cuts[0])
    for cut in cuts[1:]:
        level = level * one(*cut)
    return level


def gaussian(stream_key, dims, scale, bound, split=(), kind=jnp.bfloat16):
    level = levels(stream_key, dims, split, -0.22, 0.18) if split else 1.0
    drawn = jax.random.normal(stream_key, dims, jnp.float32) * scale * level
    return jnp.minimum(jnp.maximum(drawn, -bound), bound).astype(kind)


def setup_inputs(seed: int = 0) -> dict:
    keys = jax.random.split(jax.random.key(seed), 4)
    thermal_field = gaussian(keys[0], (ZONAL_COUNT, MERIDIONAL_COUNT, VERTICAL_COUNT), 1.0, 6.0, ((0, 4), (1, 8)), jnp.float32)
    generator_keys = place_ends(jax.random.randint(keys[1], (6,), 0, 1048576), jax.random.fold_in(keys[1], 1), 0, 1048575).astype(jnp.int32)
    slab_top_offset = jax.random.randint(keys[2], (1,), 0, 2048).astype(jnp.int32)
    return {"thermal_field": thermal_field, "generator_keys": generator_keys, "slab_top_offset": slab_top_offset}


def random_signs(seed_value, cell_index, column_index):
    hashed = cell_index * 73856093 + column_index * 19349663 + seed_value * 83492791
    hashed = jnp.bitwise_xor(hashed, lax.shift_right_logical(hashed, jnp.full_like(hashed, 15)))
    hashed = hashed * 668265261
    hashed = jnp.bitwise_xor(hashed, lax.shift_right_logical(hashed, jnp.full_like(hashed, 13)))
    parity = jnp.bitwise_and(lax.shift_right_logical(hashed, jnp.full_like(hashed, 7)), jnp.full_like(hashed, 1))
    return jnp.where(parity == 1, 1.0, -1.0).astype(jnp.float32)

def reference(thermal_field, generator_keys, slab_top_offset):
    exact_matmul_mode = lax.Precision.HIGHEST
    x_index = jnp.arange(ZONAL_COUNT, dtype=jnp.int32)[:, None]
    y_index = jnp.arange(MERIDIONAL_COUNT, dtype=jnp.int32)[:, None]
    z_index = (slab_top_offset[0] + jnp.arange(VERTICAL_COUNT, dtype=jnp.int32))[:, None]
    rank_cols = jnp.arange(RANK, dtype=jnp.int32)[None, :]
    core_cols = jnp.arange(TARGET_RANK, dtype=jnp.int32)[None, :]
    omega_x = random_signs(generator_keys[0], x_index, rank_cols)
    omega_y = random_signs(generator_keys[1], y_index, rank_cols)
    omega_z = random_signs(generator_keys[2], z_index, rank_cols)
    zonal_compressed = random_signs(generator_keys[3], x_index, core_cols)
    phi_y = random_signs(generator_keys[4], y_index, core_cols)
    phi_z = random_signs(generator_keys[5], z_index, core_cols)
    unrolled_grid = thermal_field.reshape(ZONAL_COUNT * MERIDIONAL_COUNT, VERTICAL_COUNT)
    reduced = jnp.dot(unrolled_grid, omega_z, precision=exact_matmul_mode).reshape(ZONAL_COUNT, MERIDIONAL_COUNT, RANK)
    factor_x = jnp.einsum('xyk,yk->xk', reduced, omega_y, precision=exact_matmul_mode) * (1.0 / math.sqrt(MERIDIONAL_COUNT * VERTICAL_COUNT))
    factor_y = jnp.einsum('xyk,xk->yk', reduced, omega_x, precision=exact_matmul_mode) * (1.0 / math.sqrt(ZONAL_COUNT * VERTICAL_COUNT))
    khatri = (omega_x[:, None, :] * omega_y[None, :, :]).reshape(ZONAL_COUNT * MERIDIONAL_COUNT, RANK)
    factor_z = jnp.einsum('pz,pk->zk', unrolled_grid, khatri, precision=exact_matmul_mode) * (1.0 / math.sqrt(ZONAL_COUNT * MERIDIONAL_COUNT))
    front_portion = jnp.dot(zonal_compressed.T, thermal_field.reshape(ZONAL_COUNT, MERIDIONAL_COUNT * VERTICAL_COUNT), precision=exact_matmul_mode).reshape(TARGET_RANK, MERIDIONAL_COUNT, VERTICAL_COUNT)
    second = jnp.einsum('ayz,yb->abz', front_portion, phi_y, precision=exact_matmul_mode)
    core = jnp.einsum('abz,zc->abc', second, phi_z, precision=exact_matmul_mode) * (1.0 / math.sqrt(ZONAL_COUNT * MERIDIONAL_COUNT * VERTICAL_COUNT))
    return (factor_x, factor_y, factor_z, core)
```

```python
import functools
import math

import jax
import jax.numpy as jnp
from jax import lax
from jax.experimental import pallas as pl
from jax.experimental.pallas import tpu as pltpu
from jax.sharding import PartitionSpec as P

RANK = 64
TARGET_RANK = 128


def random_signs(seed_value, cell_index, column_index):
    hashed = cell_index * 73856093 + column_index * 19349663 + seed_value * 83492791
    hashed = jnp.bitwise_xor(hashed, lax.shift_right_logical(hashed, jnp.full_like(hashed, 15)))
    hashed = hashed * 668265261
    hashed = jnp.bitwise_xor(hashed, lax.shift_right_logical(hashed, jnp.full_like(hashed, 13)))
    parity = jnp.bitwise_and(
        lax.shift_right_logical(hashed, jnp.full_like(hashed, 7)), jnp.full_like(hashed, 1)
    )
    return jnp.where(parity == 1, 1.0, -1.0).astype(jnp.float32)


def body(thermal_field, generator_keys, slab_top_offset):
    exact_matmul_mode = lax.Precision.HIGHEST
    front_length, back_length, vertical_layer = thermal_field.shape
    devices_first = lax.axis_size("gx")
    devices_second = lax.axis_size("gy")
    total_first = front_length * devices_first
    total_second = back_length * devices_second
    x_index = (lax.axis_index("gx") * front_length + jnp.arange(front_length, dtype=jnp.int32))[
        :, None
    ]
    y_index = (lax.axis_index("gy") * back_length + jnp.arange(back_length, dtype=jnp.int32))[
        :, None
    ]
    z_index = (slab_top_offset[0] + jnp.arange(vertical_layer, dtype=jnp.int32))[:, None]
    rank_cols = jnp.arange(RANK, dtype=jnp.int32)[None, :]
    core_cols = jnp.arange(TARGET_RANK, dtype=jnp.int32)[None, :]
    omega_x = random_signs(generator_keys[0], x_index, rank_cols)
    omega_y = random_signs(generator_keys[1], y_index, rank_cols)
    omega_z = random_signs(generator_keys[2], z_index, rank_cols)
    phi_xt = random_signs(generator_keys[3], x_index, core_cols).T
    phi_yt = random_signs(generator_keys[4], y_index, core_cols).T
    phi_z = random_signs(generator_keys[5], z_index, core_cols)
    unrolled_grid = thermal_field.reshape(front_length * back_length, vertical_layer)
    reduced = jnp.dot(unrolled_grid, omega_z, precision=exact_matmul_mode).reshape(
        front_length, back_length, RANK
    )
    partial_x = jnp.einsum("xyk,yk->xk", reduced, omega_y, precision=exact_matmul_mode)
    partial_y = jnp.einsum("xyk,xk->yk", reduced, omega_x, precision=exact_matmul_mode)
    khatri = (omega_x[:, None, :] * omega_y[None, :, :]).reshape(front_length * back_length, RANK)
    partial_z = jnp.einsum("pz,pk->zk", unrolled_grid, khatri, precision=exact_matmul_mode)
    summed_x, half_z = lax.psum((partial_x, partial_z), "gy")
    summed_y, summed_z = lax.psum((partial_y, half_z), "gx")
    factor_x = summed_x * (1.0 / math.sqrt(total_second * vertical_layer))
    factor_y = summed_y * (1.0 / math.sqrt(total_first * vertical_layer))
    factor_z = summed_z * (1.0 / math.sqrt(total_first * total_second))
    thermal_matrix = thermal_field.reshape(front_length, back_length * vertical_layer)
    chosen_entries = phi_xt
    reduced_first = lax.psum_scatter(
        jnp.dot(chosen_entries, thermal_matrix, precision=exact_matmul_mode),
        "gx",
        scatter_dimension=0,
        tiled=True,
    )
    reduced_first = reduced_first.reshape(-1, back_length, vertical_layer)
    chosen_entries = phi_yt
    middle = jnp.einsum("by,ayz->baz", chosen_entries, reduced_first, precision=exact_matmul_mode)
    swapped = lax.psum_scatter(
        jnp.einsum("baz,zc->bac", middle, phi_z, precision=exact_matmul_mode),
        "gy",
        scatter_dimension=0,
        tiled=True,
    )
    core_block = jnp.transpose(swapped, (1, 0, 2))
    core = core_block * (1.0 / math.sqrt(total_first * total_second * vertical_layer))
    return (factor_x, factor_y, factor_z, core)


SUB = 8
LANES = 128
PARTS = 2
MESH_ID = pl.DeviceIdType.MESH


def signs(seed_value, cell_index, column_index):
    hashed = cell_index * 73856093 + column_index * 19349663 + seed_value * 83492791
    hashed = hashed ^ lax.shift_right_logical(hashed, jnp.full_like(hashed, 15))
    hashed = hashed * 668265261
    hashed = hashed ^ lax.shift_right_logical(hashed, jnp.full_like(hashed, 13))
    return jnp.where((hashed & 128) != 0, 1.0, -1.0).astype(jnp.float32)


def iota(shape, axis):
    return lax.broadcasted_iota(jnp.int32, shape, axis)


def split(value):
    high = value.astype(jnp.bfloat16)
    low = (value - high.astype(jnp.float32)).astype(jnp.bfloat16)
    return high, low


def mm(left, right):
    return jnp.dot(left, right, preferred_element_type=jnp.float32)


def flip(index, bit):
    return index + bit - 2 * bit * ((index // bit) % 2)


def way_of(group, groups, core):
    if 2 * group + 1 == groups:
        return core
    return 0 if 2 * group < groups else 1


def step_x(ix, way, turn):
    low = flip(ix, 1)
    high = flip(ix, 2)
    first = low + (high - low) * way
    return first if turn == 0 else low + high - first


def kernel(
    dims,
    keys_in, top, field_in,
    out_x, out_y, out_z, out_core,
    keys, field, load_sem, raw_out, raw_in, spread, landed, own, near, keep, part_out, part_in,
    first_w, second_w, phi_y, phi_z,
    small_out, small_in, small_sum, zsum_in, zx_out, zx_in, fy_out, fy_in,
    s0, r0, s5, r5, s1, r1, s2, r2, s3, r3, t1, u1, t2, u2, t3, u3, t4, u4,
):
    nx, ng, front, back, depth = dims
    nz = ng // 2
    blk_a = TARGET_RANK // nx
    pairs = blk_a // 2
    out_b = TARGET_RANK // ng
    ix = lax.axis_index("gx")
    ig = lax.axis_index("gy")
    iz, core = ig // 2, ig % 2

    def dev_x(d):
        r = ix
        for bit in (1, 2):
            if d & bit:
                r = flip(r, bit)
        return r

    def dev_g(d):
        r = ig
        for bit in (1, 2, 4):
            if d & bit:
                r = flip(r, bit)
        return r

    def copy(src, dst, send, recv, dx, dg):
        return pltpu.make_async_remote_copy(
            src_ref=src, dst_ref=dst, send_sem=send, recv_sem=recv,
            device_id=(dev_x(dx), dev_g(dg)), device_id_type=MESH_ID,
        )

    load = pltpu.make_async_copy(field_in, field, load_sem.at[0])
    load.start()
    load_keys = pltpu.make_async_copy(keys_in, keys, load_sem.at[1])
    load_keys.start()
    partners = [(dx, dc) for dx in range(nx) for dc in range(2) if dx or dc]
    partners += [(0, dg) for dg in range(2, ng)]
    barrier = pltpu.get_barrier_semaphore()
    for dx, dg in partners:
        pl.semaphore_signal(
            barrier, inc=1, device_id=(dev_x(dx), dev_g(dg)), device_id_type=MESH_ID
        )

    x0 = ix * front
    y0 = ig * back
    groups = back // SUB
    order = list(range(0, groups, 2)) + list(range(1, groups, 2))
    fold = front // 2
    deep = depth // 2
    two_d = field.reshape(front * back, depth)
    lower = iota((fold, SUB, depth), 2) < deep
    load.wait()
    for h in range(2):
        for g in range(groups):
            here = field[0:fold, g * SUB : (g + 1) * SUB, :]
            there = field[fold:front, g * SUB : (g + 1) * SUB, :]
            if h == 0:
                raw_out[h, g] = jnp.where(lower, here, pltpu.roll(there, deep, 2))
            else:
                raw_out[h, g] = jnp.where(lower, pltpu.roll(here, deep, 2), there)
    pl.semaphore_wait(barrier, len(partners))
    raws = {}
    for h in range(2):
        for g in order:
            raws[h, g] = pltpu.make_async_remote_copy(
                src_ref=raw_out.at[h, g], dst_ref=raw_in.at[h, g],
                send_sem=s0.at[h, g], recv_sem=r0.at[h, g],
                device_id=(step_x(ix, way_of(g, groups, core), 0), ig), device_id_type=MESH_ID,
            )
            raws[h, g].start()
    pend = list(raws.values())
    load_keys.wait()
    z0 = top[0]

    lane = iota((RANK, 2 * front), 1)
    left = signs(
        keys[0], jnp.where(lane >= front, lane - front, lane) + x0, iota((RANK, 2 * front), 0)
    ).astype(jnp.bfloat16)
    omega_yt = signs(keys[1], iota((RANK, back), 1) + y0, iota((RANK, back), 0))
    total_z = jnp.zeros((RANK, depth), jnp.float32)
    for y in range(back):
        high, low = split(two_d[pl.ds(y, front, stride=back), :])
        both = mm(left, jnp.concatenate([high, low], axis=0))
        total_z = total_z + both * omega_yt[:, y : y + 1]

    lane_z = iota((depth, LANES), 1)
    row_z = iota((depth, LANES), 0) + z0
    omega_z = signs(keys[2], row_z, lane_z).astype(jnp.bfloat16)
    high, low = split(two_d[...])
    reduced = (mm(high, omega_z) + mm(low, omega_z)).reshape(front, back, LANES)
    omega_y = signs(keys[1], iota((back, LANES), 0) + y0, iota((back, LANES), 1))
    part_y = jnp.zeros((back, LANES), jnp.float32)
    omega_x = signs(keys[0], iota((front, LANES), 0) + x0, iota((front, LANES), 1))
    part_x = jnp.sum(reduced * omega_y[None], axis=1)
    for x in range(front):
        part_y = part_y + reduced[x] * omega_x[x : x + 1]
    fy_out[...] = part_y
    per = front // ng
    kper = RANK // ng
    for d in range(ng):
        small_out[d, 0:kper] = total_z[d * kper : (d + 1) * kper]
        small_out[d, SUB : SUB + per] = part_x[d * per : (d + 1) * per]
    fy = []
    for d in range(1, nx):
        fy.append(copy(fy_out, fy_in.at[d - 1], t1.at[d - 1], u1.at[d - 1], d, 0))
        fy[-1].start()
    sm = []
    for d in range(1, ng):
        sm.append(copy(
            small_out.at[dev_g(d)], small_in.at[d - 1], t2.at[d - 1], u2.at[d - 1], 0, d
        ))
        sm[-1].start()
    pend += fy

    def weights(base, far_x):
        shape = (4 * pairs, 4 * fold)
        row = iota(shape, 0)
        lane = iota(shape, 1)
        lane = jnp.where(lane >= front, lane - front, lane)
        second = row >= 2 * pairs
        row = jnp.where(second, row - 2 * pairs, row)
        swapped = jnp.where(lane >= fold, lane - fold, lane + fold)
        cell = jnp.where(second, swapped, lane) + base
        target = jnp.where(row < pairs, ix * blk_a, far_x * blk_a - pairs) + row
        target = jnp.where(second, target + pairs, target)
        return signs(keys[3], cell, target).astype(jnp.bfloat16)

    for g in range(groups):
        way = way_of(g, groups, core)
        first_w[g] = weights(x0, step_x(ix, way, 1))
        second_w[g] = weights(step_x(ix, way, 0) * front, step_x(ix, way, 1))

    lower_row = iota((2 * pairs, depth), 1) < deep

    def contract(left, packed):
        both = jnp.concatenate([packed, pltpu.roll(packed, deep, 1)], axis=0)
        high, low = split(both)
        out = mm(left, jnp.concatenate([high, low], axis=0))
        return jnp.where(lower_row, out[: 2 * pairs], out[2 * pairs :])

    for h in range(2):
        wide = spread.at[h].reshape(2 * pairs * back, depth)
        for g in order:
            flat = raw_out.at[h, g].reshape(fold * SUB, depth)
            for y in range(SUB):
                wide[pl.ds(g * SUB + y, 2 * pairs, stride=back), :] = contract(
                    first_w[g], flat[pl.ds(y, fold, stride=SUB), :]
                )

    shape = (4 * out_b, 4 * back)
    row = iota(shape, 0)
    col = iota(shape, 1)
    col = jnp.where(col >= 2 * back, col - 2 * back, col)
    target = row
    for k, d in enumerate((0, 1, 4, 5)):
        target = jnp.where(row >= k * out_b, row + (dev_g(d) - k) * out_b, target)
    for src in range(2):
        cell = jnp.where(col >= back, dev_g(2 * src + 1) * back - back, dev_g(2 * src) * back) + col
        phi_y[:, src * 4 * back : (src + 1) * 4 * back] = signs(keys[4], cell, target).astype(
            jnp.bfloat16
        )
    row = iota((depth, 2 * LANES), 0)
    col = iota((depth, 2 * LANES), 1)
    same = (row >= deep) == (col >= LANES)
    row = jnp.where(row >= deep, row - deep, row) + z0
    col = jnp.where(col >= LANES, col - LANES, col)
    for h in range(2):
        phi_z[h] = jnp.where(same, signs(keys[5], row + h * deep, col), 0.0).astype(jnp.bfloat16)

    def receive_raw(h):
        wide = spread.at[h].reshape(2 * pairs * back, depth)
        sends = []
        for g in order:
            raws[h, g].wait_recv()
            flat = raw_in.at[h, g].reshape(fold * SUB, depth)
            for y in range(SUB):
                place = pl.ds(g * SUB + y, 2 * pairs, stride=back)
                wide[place, :] = wide[place, :] + contract(
                    second_w[g], flat[pl.ds(y, fold, stride=SUB), :]
                )
            for dc in (1, 0):
                start = pairs + (dev_g(dc) % 2) * SUB
                sends.append(pltpu.make_async_remote_copy(
                    src_ref=spread.at[h, pl.ds(start, SUB), g * SUB : (g + 1) * SUB, :],
                    dst_ref=landed.at[h, dc, :, g * SUB : (g + 1) * SUB, :],
                    send_sem=s1.at[h, dc, g], recv_sem=r1.at[h, dc, g],
                    device_id=(step_x(ix, way_of(g, groups, core), 1), dev_g(dc)),
                    device_id_type=MESH_ID,
                ))
                sends[-1].start()
        sends.append(copy(
            spread.at[h, pl.ds((1 - core) * SUB, SUB)], landed.at[h, 2], s5.at[h], r5.at[h], 0, 1
        ))
        sends[-1].start()
        return sends

    rows = SUB // PARTS
    nearby = {}

    def send_near(h, sends):
        for c in sends:
            c.wait_recv()
        for p in range(PARTS):
            at = slice(p * rows, (p + 1) * rows)
            own[h, at, 0] = spread[h, pl.ds(core * SUB + p * rows, rows)] + landed[h, 0, at]
            own[h, at, 1] = landed[h, 2, at] + landed[h, 1, at]
            nearby[h, p] = copy(
                own.at[h, at], near.at[h, at], s2.at[h, p], r2.at[h, p], 0, 2
            )
            nearby[h, p].start()

    first = receive_raw(0)
    for c in sm:
        c.wait_recv()
    block = small_out[ig]
    for d in range(1, ng):
        block = block + small_in[d - 1]
    small_sum[...] = block
    zx = []
    for d in range(1, nx):
        zx.append(copy(
            small_sum.at[0:SUB], zsum_in.at[d - 1], t3.at[d - 1], u3.at[d - 1], d, 0
        ))
        zx[-1].start()
    second = receive_raw(1)
    for c in zx:
        c.wait_recv()
    zpart = small_sum[0:SUB]
    for d in range(1, nx):
        zpart = zpart + zsum_in[d - 1]
    zx_out[0:SUB] = zpart
    zx_out[SUB:] = small_sum[SUB:]
    gathered = []
    for d in range(1, ng):
        gathered.append(copy(zx_out, zx_in.at[d - 1], t4.at[d - 1], u4.at[d - 1], 0, d))
        gathered[-1].start()
    send_near(0, first)
    send_near(1, second)
    pend += first + second + zx + gathered + list(nearby.values())

    parts = {}
    for h in range(2):
        for p in range(PARTS):
            nearby[h, p].wait_recv()
            for r in range(rows):
                at = p * rows + r
                pieces = split(own[h, at].reshape(2 * back, depth))
                pieces += split(near[h, at].reshape(2 * back, depth))
                total = mm(phi_y[...], jnp.concatenate(pieces, axis=0))
                keep[h, at] = total[:out_b]
                for k in range(3):
                    part_out[h, p, k, r] = total[(k + 1) * out_b : (k + 2) * out_b]
            for k, d in ((1, 4), (2, 5), (0, 1)):
                parts[h, p, k] = copy(
                    part_out.at[h, p, k], part_in.at[h, p, k], s3.at[h, p, k], r3.at[h, p, k], 0, d
                )
                parts[h, p, k].start()
    pend += list(parts.values())

    for c in fy:
        c.wait_recv()
    value = fy_out[...]
    for d in range(1, nx):
        value = value + fy_in[d - 1]
    out_y[...] = (value * (1.0 / math.sqrt(front * nx * depth)))[:, :RANK]
    for c in gathered:
        c.wait_recv()
    for c in sm:
        c.wait_send()
    for d in range(ng):
        block = zx_out[...] if d == 0 else zx_in[d - 1]
        small_out[dev_g(d)] = block
    scale_x = 1.0 / math.sqrt(back * ng * depth)
    scale_z = 1.0 / math.sqrt(front * nx * back * ng)
    for d in range(ng):
        out_x[d * per : (d + 1) * per, :] = small_out[d, SUB : SUB + per, :RANK] * scale_x
        out_z[d * kper : (d + 1) * kper, :] = small_out[d, 0:kper] * scale_z

    scale = 1.0 / math.sqrt(front * nx * back * ng * depth)
    count = rows * out_b
    for h in range(2):
        for p in range(PARTS):
            for k in range(3):
                parts[h, p, k].wait_recv()
            at = slice(p * rows, (p + 1) * rows)
            mine = (keep[h, at] + part_in[h, p, 1]).reshape(count, depth)
            other = (part_in[h, p, 0] + part_in[h, p, 2]).reshape(count, depth)
            high, low = split(jnp.concatenate([mine, other], axis=0))
            value = (mm(high, phi_z[h]) + mm(low, phi_z[h])) * scale
            for i in range(2):
                for which in range(2):
                    side = core if which == 0 else 1 - core
                    start = pl.multiple_of((i * pairs + side * SUB + p * rows) * out_b, SUB)
                    place = pl.ds(start, count)
                    piece = value[which * count : (which + 1) * count, i * LANES : (i + 1) * LANES]
                    out_core[place, :] = piece if h == 0 else out_core[place, :] + piece
    for c in pend:
        c.wait_send()


def publish(*refs):
    ready, out, sems = refs[:4], refs[4:8], refs[8]
    copies = [pltpu.make_async_copy(a, b, sems.at[i]) for i, (a, b) in enumerate(zip(ready, out))]
    for c in copies:
        c.start()
    for c in copies:
        c.wait()


def fused_body(nx, ng, thermal_field, generator_keys, slab_top_offset):
    front, back, depth = thermal_field.shape
    blk_a = TARGET_RANK // nx
    out_b = TARGET_RANK // ng
    f32 = jnp.float32
    bf16 = jnp.bfloat16
    vmem = pltpu.VMEM
    dma = pltpu.SemaphoreType.DMA
    groups = back // SUB
    rows = SUB // PARTS
    scratch = [
        pltpu.SMEM(generator_keys.shape, jnp.int32),
        vmem((front, back, depth), f32),
        dma((2,)),
        vmem((2, groups, front // 2, SUB, depth), f32),
        vmem((2, groups, front // 2, SUB, depth), f32),
        vmem((2, blk_a, back, depth), f32),
        vmem((2, 3, SUB, back, depth), f32),
        vmem((2, SUB, 2, back, depth), f32),
        vmem((2, SUB, 2, back, depth), f32),
        vmem((2, SUB, out_b, depth), f32),
        vmem((2, PARTS, 3, rows, out_b, depth), f32),
        vmem((2, PARTS, 3, rows, out_b, depth), f32),
        vmem((groups, 2 * blk_a, 2 * front), bf16),
        vmem((groups, 2 * blk_a, 2 * front), bf16),
        vmem((4 * out_b, 8 * back), bf16),
        vmem((2, depth, 2 * LANES), bf16),
        vmem((ng, 2 * SUB, LANES), f32),
        vmem((ng - 1, 2 * SUB, LANES), f32),
        vmem((2 * SUB, LANES), f32),
        vmem((nx - 1, SUB, LANES), f32),
        vmem((2 * SUB, LANES), f32),
        vmem((ng - 1, 2 * SUB, LANES), f32),
        vmem((back, LANES), f32),
        vmem((nx - 1, back, LANES), f32),
        dma((2, groups)), dma((2, groups)),
        dma((2,)), dma((2,)),
        dma((2, 2, groups)), dma((2, 2, groups)),
        dma((2, PARTS)), dma((2, PARTS)),
        dma((2, PARTS, 3)), dma((2, PARTS, 3)),
        dma((nx - 1,)), dma((nx - 1,)),
        dma((ng - 1,)), dma((ng - 1,)),
        dma((nx - 1,)), dma((nx - 1,)),
        dma((ng - 1,)), dma((ng - 1,)),
    ]
    whole = pl.BlockSpec(memory_space=pltpu.VMEM)
    far = pl.BlockSpec(memory_space=pltpu.HBM)
    shapes = (
        jax.ShapeDtypeStruct((front, RANK), f32),
        jax.ShapeDtypeStruct((back, RANK), f32),
        jax.ShapeDtypeStruct((RANK, depth), f32),
        jax.ShapeDtypeStruct((blk_a * out_b, depth), f32),
    )
    def stay(array):
        return pltpu.with_memory_space_constraint(array, pltpu.HBM)

    results = pl.pallas_call(
        functools.partial(kernel, (nx, ng, front, back, depth)),
        out_shape=shapes,
        in_specs=[far, pl.BlockSpec(memory_space=pltpu.SMEM), far],
        out_specs=(whole,) * 4,
        scratch_shapes=scratch,
        compiler_params=pltpu.CompilerParams(
            collective_id=0, has_side_effects=True, vmem_limit_bytes=40 * 2**20
        ),
    )(stay(generator_keys), slab_top_offset, stay(thermal_field))
    fx, fy, fz, core = pl.pallas_call(
        publish,
        out_shape=shapes,
        in_specs=[whole] * 4,
        out_specs=(far,) * 4,
        scratch_shapes=[dma((4,))],
        compiler_params=pltpu.CompilerParams(vmem_limit_bytes=2**20),
    )(*results)
    return fx, fy, fz.T, core.reshape(blk_a, out_b, depth)


def suits(nx, ng):
    return nx == 4 and ng == 8


def solution(mesh):
    nx, ng = mesh.shape["gx"], mesh.shape["gy"]
    chosen = functools.partial(fused_body, nx, ng) if suits(nx, ng) else body
    placed = (P("gx", "gy", None), P(), P())
    return jax.shard_map(
        chosen,
        mesh=mesh,
        in_specs=placed,
        out_specs=(P("gx", None), P("gy", None), P(), P("gx", "gy", None)),
        check_vma=False,
    )
```

```python
import functools
import math

import jax
import jax.numpy as jnp
from jax import lax
from jax.experimental import pallas as pl
from jax.experimental.pallas import tpu as pltpu
from jax.sharding import PartitionSpec as P

RANK = 64
TARGET_RANK = 128


def random_signs(seed_value, cell_index, column_index):
    hashed = cell_index * 73856093 + column_index * 19349663 + seed_value * 83492791
    hashed = jnp.bitwise_xor(hashed, lax.shift_right_logical(hashed, jnp.full_like(hashed, 15)))
    hashed = hashed * 668265261
    hashed = jnp.bitwise_xor(hashed, lax.shift_right_logical(hashed, jnp.full_like(hashed, 13)))
    parity = jnp.bitwise_and(
        lax.shift_right_logical(hashed, jnp.full_like(hashed, 7)), jnp.full_like(hashed, 1)
    )
    return jnp.where(parity == 1, 1.0, -1.0).astype(jnp.float32)


def body(thermal_field, generator_keys, slab_top_offset):
    exact_matmul_mode = lax.Precision.HIGHEST
    front_length, back_length, vertical_layer = thermal_field.shape
    devices_first = lax.axis_size("gx")
    devices_second = lax.axis_size("gy")
    total_first = front_length * devices_first
    total_second = back_length * devices_second
    x_index = (lax.axis_index("gx") * front_length + jnp.arange(front_length, dtype=jnp.int32))[
        :, None
    ]
    y_index = (lax.axis_index("gy") * back_length + jnp.arange(back_length, dtype=jnp.int32))[
        :, None
    ]
    z_index = (slab_top_offset[0] + jnp.arange(vertical_layer, dtype=jnp.int32))[:, None]
    rank_cols = jnp.arange(RANK, dtype=jnp.int32)[None, :]
    core_cols = jnp.arange(TARGET_RANK, dtype=jnp.int32)[None, :]
    omega_x = random_signs(generator_keys[0], x_index, rank_cols)
    omega_y = random_signs(generator_keys[1], y_index, rank_cols)
    omega_z = random_signs(generator_keys[2], z_index, rank_cols)
    phi_xt = random_signs(generator_keys[3], x_index, core_cols).T
    phi_yt = random_signs(generator_keys[4], y_index, core_cols).T
    phi_z = random_signs(generator_keys[5], z_index, core_cols)
    unrolled_grid = thermal_field.reshape(front_length * back_length, vertical_layer)
    reduced = jnp.dot(unrolled_grid, omega_z, precision=exact_matmul_mode).reshape(
        front_length, back_length, RANK
    )
    partial_x = jnp.einsum("xyk,yk->xk", reduced, omega_y, precision=exact_matmul_mode)
    partial_y = jnp.einsum("xyk,xk->yk", reduced, omega_x, precision=exact_matmul_mode)
    khatri = (omega_x[:, None, :] * omega_y[None, :, :]).reshape(front_length * back_length, RANK)
    partial_z = jnp.einsum("pz,pk->zk", unrolled_grid, khatri, precision=exact_matmul_mode)
    summed_x, half_z = lax.psum((partial_x, partial_z), "gy")
    summed_y, summed_z = lax.psum((partial_y, half_z), "gx")
    factor_x = summed_x * (1.0 / math.sqrt(total_second * vertical_layer))
    factor_y = summed_y * (1.0 / math.sqrt(total_first * vertical_layer))
    factor_z = summed_z * (1.0 / math.sqrt(total_first * total_second))
    thermal_matrix = thermal_field.reshape(front_length, back_length * vertical_layer)
    chosen_entries = phi_xt
    reduced_first = lax.psum_scatter(
        jnp.dot(chosen_entries, thermal_matrix, precision=exact_matmul_mode),
        "gx",
        scatter_dimension=0,
        tiled=True,
    )
    reduced_first = reduced_first.reshape(-1, back_length, vertical_layer)
    chosen_entries = phi_yt
    middle = jnp.einsum("by,ayz->baz", chosen_entries, reduced_first, precision=exact_matmul_mode)
    swapped = lax.psum_scatter(
        jnp.einsum("baz,zc->bac", middle, phi_z, precision=exact_matmul_mode),
        "gy",
        scatter_dimension=0,
        tiled=True,
    )
    core_block = jnp.transpose(swapped, (1, 0, 2))
    core = core_block * (1.0 / math.sqrt(total_first * total_second * vertical_layer))
    return (factor_x, factor_y, factor_z, core)


SUB = 8
LANES = 128
PARTS = 2
MESH_ID = pl.DeviceIdType.MESH


def signs(seed_value, cell_index, column_index):
    hashed = cell_index * 73856093 + column_index * 19349663 + seed_value * 83492791
    hashed = hashed ^ lax.shift_right_logical(hashed, jnp.full_like(hashed, 15))
    hashed = hashed * 668265261
    hashed = hashed ^ lax.shift_right_logical(hashed, jnp.full_like(hashed, 13))
    return jnp.where((hashed & 128) != 0, 1.0, -1.0).astype(jnp.float32)


def iota(shape, axis):
    return lax.broadcasted_iota(jnp.int32, shape, axis)


def split(value):
    high = value.astype(jnp.bfloat16)
    low = (value - high.astype(jnp.float32)).astype(jnp.bfloat16)
    return high, low


def mm(left, right):
    return jnp.dot(left, right, preferred_element_type=jnp.float32)


def flip(index, bit):
    return index + bit - 2 * bit * ((index // bit) % 2)


def way_of(group, groups, half):
    if 2 * group + 1 == groups:
        return half
    return 0 if 2 * group < groups else 1


def step_x(ix, way, turn):
    low = flip(ix, 1)
    high = flip(ix, 2)
    first = low + (high - low) * way
    return first if turn == 0 else low + high - first


def kernel(
    dims,
    keys_in, top, field_in,
    out_x, out_y, out_z, out_core,
    keys, field, load_sem, raw_out, raw_in, spread, landed, own, near, keep, part_out, part_in,
    first_w, second_w, phi_y, phi_z,
    small_out, small_in, small_sum, zsum_in, zx_out, zx_in, fy_out, fy_in,
    s0, r0, s5, r5, s1, r1, s2, r2, s3, r3, t1, u1, t2, u2, t3, u3, t4, u4,
):
    nx, ng, front, back, depth = dims
    nz = ng // 2
    blk_a = TARGET_RANK // nx
    pairs = blk_a // 2
    out_b = TARGET_RANK // ng
    ix = lax.axis_index("gx")
    ig = lax.axis_index("gy")
    iz, core = ig // 2, ig % 2

    def dev_x(d):
        r = ix
        for bit in (1, 2):
            if d & bit:
                r = flip(r, bit)
        return r

    def dev_g(d):
        r = ig
        for bit in (1, 2, 4):
            if d & bit:
                r = flip(r, bit)
        return r

    def copy(src, dst, send, recv, dx, dg):
        return pltpu.make_async_remote_copy(
            src_ref=src, dst_ref=dst, send_sem=send, recv_sem=recv,
            device_id=(dev_x(dx), dev_g(dg)), device_id_type=MESH_ID,
        )

    load = pltpu.make_async_copy(field_in, field, load_sem.at[0])
    load.start()
    load_keys = pltpu.make_async_copy(keys_in, keys, load_sem.at[1])
    load_keys.start()
    partners = [(dx, dc) for dx in range(nx) for dc in range(2) if dx or dc]
    partners += [(0, dg) for dg in range(2, ng)]
    barrier = pltpu.get_barrier_semaphore()
    for dx, dg in partners:
        pl.semaphore_signal(
            barrier, inc=1, device_id=(dev_x(dx), dev_g(dg)), device_id_type=MESH_ID
        )

    x0 = ix * front
    y0 = ig * back
    groups = back // SUB
    order = list(range(0, groups, 2)) + list(range(1, groups, 2))
    fold = front // 2
    deep = depth // 2
    two_d = field.reshape(front * back, depth)
    lower = iota((fold, SUB, depth), 2) < deep
    load.wait()
    for h in range(2):
        for g in range(groups):
            here = field[0:fold, g * SUB : (g + 1) * SUB, :]
            there = field[fold:front, g * SUB : (g + 1) * SUB, :]
            if h == 0:
                raw_out[h, g] = jnp.where(lower, here, pltpu.roll(there, deep, 2))
            else:
                raw_out[h, g] = jnp.where(lower, pltpu.roll(here, deep, 2), there)
    pl.semaphore_wait(barrier, len(partners))
    raws = {}
    for h in range(2):
        for g in order:
            raws[h, g] = pltpu.make_async_remote_copy(
                src_ref=raw_out.at[h, g], dst_ref=raw_in.at[h, g],
                send_sem=s0.at[h, g], recv_sem=r0.at[h, g],
                device_id=(step_x(ix, way_of(g, groups, h), 0), ig), device_id_type=MESH_ID,
            )
            raws[h, g].start()
    pend = list(raws.values())
    load_keys.wait()
    z0 = top[0]

    lane = iota((RANK, 2 * front), 1)
    left = signs(
        keys[0], jnp.where(lane >= front, lane - front, lane) + x0, iota((RANK, 2 * front), 0)
    ).astype(jnp.bfloat16)
    omega_yt = signs(keys[1], iota((RANK, back), 1) + y0, iota((RANK, back), 0))
    total_z = jnp.zeros((RANK, depth), jnp.float32)
    for y in range(back):
        high, low = split(two_d[pl.ds(y, front, stride=back), :])
        both = mm(left, jnp.concatenate([high, low], axis=0))
        total_z = total_z + both * omega_yt[:, y : y + 1]

    lane_z = iota((depth, LANES), 1)
    row_z = iota((depth, LANES), 0) + z0
    omega_z = signs(keys[2], row_z, lane_z).astype(jnp.bfloat16)
    high, low = split(two_d[...])
    reduced = (mm(high, omega_z) + mm(low, omega_z)).reshape(front, back, LANES)
    omega_y = signs(keys[1], iota((back, LANES), 0) + y0, iota((back, LANES), 1))
    part_y = jnp.zeros((back, LANES), jnp.float32)
    omega_x = signs(keys[0], iota((front, LANES), 0) + x0, iota((front, LANES), 1))
    part_x = jnp.sum(reduced * omega_y[None], axis=1)
    for x in range(front):
        part_y = part_y + reduced[x] * omega_x[x : x + 1]
    fy_out[...] = part_y
    per = front // ng
    kper = RANK // ng
    for d in range(ng):
        small_out[d, 0:kper] = total_z[d * kper : (d + 1) * kper]
        small_out[d, SUB : SUB + per] = part_x[d * per : (d + 1) * per]
    sm = []
    for d in range(1, ng):
        sm.append(copy(
            small_out.at[dev_g(d)], small_in.at[d - 1], t2.at[d - 1], u2.at[d - 1], 0, d
        ))
        sm[-1].start()

    def weights(base, far_x):
        shape = (4 * pairs, 4 * fold)
        row = iota(shape, 0)
        lane = iota(shape, 1)
        lane = jnp.where(lane >= front, lane - front, lane)
        second = row >= 2 * pairs
        row = jnp.where(second, row - 2 * pairs, row)
        swapped = jnp.where(lane >= fold, lane - fold, lane + fold)
        cell = jnp.where(second, swapped, lane) + base
        target = jnp.where(row < pairs, ix * blk_a, far_x * blk_a - pairs) + row
        target = jnp.where(second, target + pairs, target)
        return signs(keys[3], cell, target).astype(jnp.bfloat16)

    for way in range(2):
        first_w[way] = weights(x0, step_x(ix, way, 1))
        second_w[way] = weights(step_x(ix, way, 0) * front, step_x(ix, way, 1))

    lower_row = iota((2 * pairs, depth), 1) < deep

    def contract(left, packed):
        both = jnp.concatenate([packed, pltpu.roll(packed, deep, 1)], axis=0)
        high, low = split(both)
        out = mm(left, jnp.concatenate([high, low], axis=0))
        return jnp.where(lower_row, out[: 2 * pairs], out[2 * pairs :])

    for h in range(2):
        wide = spread.at[h].reshape(2 * pairs * back, depth)
        for g in order:
            flat = raw_out.at[h, g].reshape(fold * SUB, depth)
            for y in range(SUB):
                wide[pl.ds(g * SUB + y, 2 * pairs, stride=back), :] = contract(
                    first_w[way_of(g, groups, h)], flat[pl.ds(y, fold, stride=SUB), :]
                )

    shape = (4 * out_b, 4 * back)
    row = iota(shape, 0)
    col = iota(shape, 1)
    col = jnp.where(col >= 2 * back, col - 2 * back, col)
    target = row
    for k, d in enumerate((0, 1, 4, 5)):
        target = jnp.where(row >= k * out_b, row + (dev_g(d) - k) * out_b, target)
    for src in range(2):
        cell = jnp.where(col >= back, dev_g(2 * src + 1) * back - back, dev_g(2 * src) * back) + col
        phi_y[:, src * 4 * back : (src + 1) * 4 * back] = signs(keys[4], cell, target).astype(
            jnp.bfloat16
        )
    row = iota((depth, 2 * LANES), 0)
    col = iota((depth, 2 * LANES), 1)
    same = (row >= deep) == (col >= LANES)
    row = jnp.where(row >= deep, row - deep, row) + z0
    col = jnp.where(col >= LANES, col - LANES, col)
    for h in range(2):
        phi_z[h] = jnp.where(same, signs(keys[5], row + h * deep, col), 0.0).astype(jnp.bfloat16)

    rows = SUB // PARTS

    def receive_raw(h):
        wide = spread.at[h].reshape(2 * pairs * back, depth)
        sends = [[] for _ in range(PARTS)]
        for g in order:
            raws[h, g].wait_recv()
            flat = raw_in.at[h, g].reshape(fold * SUB, depth)
            for y in range(SUB):
                place = pl.ds(g * SUB + y, 2 * pairs, stride=back)
                wide[place, :] = wide[place, :] + contract(
                    second_w[way_of(g, groups, h)], flat[pl.ds(y, fold, stride=SUB), :]
                )
            for p in range(PARTS):
                for dc in (1, 0):
                    start = pairs + (dev_g(dc) % 2) * SUB + p * rows
                    ys = slice(g * SUB, (g + 1) * SUB)
                    sends[p].append(pltpu.make_async_remote_copy(
                        src_ref=spread.at[h, pl.ds(start, rows), ys, :],
                        dst_ref=landed.at[h, dc, p * rows : (p + 1) * rows, ys, :],
                        send_sem=s1.at[h, p, dc, g], recv_sem=r1.at[h, p, dc, g],
                        device_id=(step_x(ix, way_of(g, groups, h), 1), dev_g(dc)),
                        device_id_type=MESH_ID,
                    ))
                    sends[p][-1].start()
        for p in range(PARTS):
            sends[p].append(copy(
                spread.at[h, pl.ds((1 - core) * SUB + p * rows, rows)],
                landed.at[h, 2, p * rows : (p + 1) * rows],
                s5.at[h, p], r5.at[h, p], 0, 1,
            ))
            sends[p][-1].start()
        return sends

    nearby = {}

    def send_near(h, sends):
        for p in range(PARTS):
            for c in sends[p]:
                c.wait_recv()
            at = slice(p * rows, (p + 1) * rows)
            own[h, at, 0] = spread[h, pl.ds(core * SUB + p * rows, rows)] + landed[h, 0, at]
            own[h, at, 1] = landed[h, 2, at] + landed[h, 1, at]
            nearby[h, p] = copy(
                own.at[h, at], near.at[h, at], s2.at[h, p], r2.at[h, p], 0, 2
            )
            nearby[h, p].start()

    first = receive_raw(0)
    for c in sm:
        c.wait_recv()
    block = small_out[ig]
    for d in range(1, ng):
        block = block + small_in[d - 1]
    small_sum[...] = block
    zx = []
    for d in range(1, nx):
        zx.append(copy(
            small_sum.at[0:SUB], zsum_in.at[d - 1], t3.at[d - 1], u3.at[d - 1], d, 0
        ))
        zx[-1].start()
    second = receive_raw(1)
    fy = []
    for d in range(1, nx):
        fy.append(copy(fy_out, fy_in.at[d - 1], t1.at[d - 1], u1.at[d - 1], d, 0))
        fy[-1].start()
    pend += fy
    for c in zx:
        c.wait_recv()
    zpart = small_sum[0:SUB]
    for d in range(1, nx):
        zpart = zpart + zsum_in[d - 1]
    zx_out[0:SUB] = zpart
    zx_out[SUB:] = small_sum[SUB:]
    gathered = []
    for d in range(1, ng):
        gathered.append(copy(zx_out, zx_in.at[d - 1], t4.at[d - 1], u4.at[d - 1], 0, d))
        gathered[-1].start()
    send_near(0, first)
    send_near(1, second)
    pend += sum(first + second, []) + zx + gathered + list(nearby.values())

    parts = {}
    for h in range(2):
        for p in range(PARTS):
            nearby[h, p].wait_recv()
            for r in range(rows):
                at = p * rows + r
                pieces = split(own[h, at].reshape(2 * back, depth))
                pieces += split(near[h, at].reshape(2 * back, depth))
                total = mm(phi_y[...], jnp.concatenate(pieces, axis=0))
                keep[h, at] = total[:out_b]
                for k in range(3):
                    part_out[h, p, k, r] = total[(k + 1) * out_b : (k + 2) * out_b]
            for k, d in ((1, 4), (2, 5), (0, 1)):
                parts[h, p, k] = copy(
                    part_out.at[h, p, k], part_in.at[h, p, k], s3.at[h, p, k], r3.at[h, p, k], 0, d
                )
                parts[h, p, k].start()
    pend += list(parts.values())

    for c in fy:
        c.wait_recv()
    value = fy_out[...]
    for d in range(1, nx):
        value = value + fy_in[d - 1]
    out_y[...] = (value * (1.0 / math.sqrt(front * nx * depth)))[:, :RANK]
    for c in gathered:
        c.wait_recv()
    for c in sm:
        c.wait_send()
    for d in range(ng):
        block = zx_out[...] if d == 0 else zx_in[d - 1]
        small_out[dev_g(d)] = block
    scale_x = 1.0 / math.sqrt(back * ng * depth)
    scale_z = 1.0 / math.sqrt(front * nx * back * ng)
    for d in range(ng):
        out_x[d * per : (d + 1) * per, :] = small_out[d, SUB : SUB + per, :RANK] * scale_x
        out_z[d * kper : (d + 1) * kper, :] = small_out[d, 0:kper] * scale_z

    scale = 1.0 / math.sqrt(front * nx * back * ng * depth)
    count = rows * out_b
    for h in range(2):
        for p in range(PARTS):
            for k in range(3):
                parts[h, p, k].wait_recv()
            at = slice(p * rows, (p + 1) * rows)
            mine = (keep[h, at] + part_in[h, p, 1]).reshape(count, depth)
            other = (part_in[h, p, 0] + part_in[h, p, 2]).reshape(count, depth)
            high, low = split(jnp.concatenate([mine, other], axis=0))
            value = (mm(high, phi_z[h]) + mm(low, phi_z[h])) * scale
            for i in range(2):
                for which in range(2):
                    side = core if which == 0 else 1 - core
                    start = pl.multiple_of((i * pairs + side * SUB + p * rows) * out_b, SUB)
                    place = pl.ds(start, count)
                    piece = value[which * count : (which + 1) * count, i * LANES : (i + 1) * LANES]
                    out_core[place, :] = piece if h == 0 else out_core[place, :] + piece
    for c in pend:
        c.wait_send()


def publish(*refs):
    ready, out, sems = refs[:4], refs[4:8], refs[8]
    copies = [pltpu.make_async_copy(a, b, sems.at[i]) for i, (a, b) in enumerate(zip(ready, out))]
    for c in copies:
        c.start()
    for c in copies:
        c.wait()


def fused_body(nx, ng, thermal_field, generator_keys, slab_top_offset):
    front, back, depth = thermal_field.shape
    blk_a = TARGET_RANK // nx
    out_b = TARGET_RANK // ng
    f32 = jnp.float32
    bf16 = jnp.bfloat16
    vmem = pltpu.VMEM
    dma = pltpu.SemaphoreType.DMA
    groups = back // SUB
    rows = SUB // PARTS
    scratch = [
        pltpu.SMEM(generator_keys.shape, jnp.int32),
        vmem((front, back, depth), f32),
        dma((2,)),
        vmem((2, groups, front // 2, SUB, depth), f32),
        vmem((2, groups, front // 2, SUB, depth), f32),
        vmem((2, blk_a, back, depth), f32),
        vmem((2, 3, SUB, back, depth), f32),
        vmem((2, SUB, 2, back, depth), f32),
        vmem((2, SUB, 2, back, depth), f32),
        vmem((2, SUB, out_b, depth), f32),
        vmem((2, PARTS, 3, rows, out_b, depth), f32),
        vmem((2, PARTS, 3, rows, out_b, depth), f32),
        vmem((2, 2 * blk_a, 2 * front), bf16),
        vmem((2, 2 * blk_a, 2 * front), bf16),
        vmem((4 * out_b, 8 * back), bf16),
        vmem((2, depth, 2 * LANES), bf16),
        vmem((ng, 2 * SUB, LANES), f32),
        vmem((ng - 1, 2 * SUB, LANES), f32),
        vmem((2 * SUB, LANES), f32),
        vmem((nx - 1, SUB, LANES), f32),
        vmem((2 * SUB, LANES), f32),
        vmem((ng - 1, 2 * SUB, LANES), f32),
        vmem((back, LANES), f32),
        vmem((nx - 1, back, LANES), f32),
        dma((2, groups)), dma((2, groups)),
        dma((2, PARTS)), dma((2, PARTS)),
        dma((2, PARTS, 2, groups)), dma((2, PARTS, 2, groups)),
        dma((2, PARTS)), dma((2, PARTS)),
        dma((2, PARTS, 3)), dma((2, PARTS, 3)),
        dma((nx - 1,)), dma((nx - 1,)),
        dma((ng - 1,)), dma((ng - 1,)),
        dma((nx - 1,)), dma((nx - 1,)),
        dma((ng - 1,)), dma((ng - 1,)),
    ]
    whole = pl.BlockSpec(memory_space=pltpu.VMEM)
    far = pl.BlockSpec(memory_space=pltpu.HBM)
    shapes = (
        jax.ShapeDtypeStruct((front, RANK), f32),
        jax.ShapeDtypeStruct((back, RANK), f32),
        jax.ShapeDtypeStruct((RANK, depth), f32),
        jax.ShapeDtypeStruct((blk_a * out_b, depth), f32),
    )
    def stay(array):
        return pltpu.with_memory_space_constraint(array, pltpu.HBM)

    results = pl.pallas_call(
        functools.partial(kernel, (nx, ng, front, back, depth)),
        out_shape=shapes,
        in_specs=[far, pl.BlockSpec(memory_space=pltpu.SMEM), far],
        out_specs=(whole,) * 4,
        scratch_shapes=scratch,
        compiler_params=pltpu.CompilerParams(
            collective_id=0, has_side_effects=True, vmem_limit_bytes=40 * 2**20
        ),
    )(stay(generator_keys), slab_top_offset, stay(thermal_field))
    fx, fy, fz, core = pl.pallas_call(
        publish,
        out_shape=shapes,
        in_specs=[whole] * 4,
        out_specs=(far,) * 4,
        scratch_shapes=[dma((4,))],
        compiler_params=pltpu.CompilerParams(vmem_limit_bytes=2**20),
    )(*results)
    return fx, fy, fz.T, core.reshape(blk_a, out_b, depth)


def suits(nx, ng):
    return nx == 4 and ng == 8


def solution(mesh):
    nx, ng = mesh.shape["gx"], mesh.shape["gy"]
    chosen = functools.partial(fused_body, nx, ng) if suits(nx, ng) else body
    placed = (P("gx", "gy", None), P(), P())
    return jax.shard_map(
        chosen,
        mesh=mesh,
        in_specs=placed,
        out_specs=(P("gx", None), P("gy", None), P(), P("gx", "gy", None)),
        check_vma=False,
    )
```

```python
import functools
import math

import jax
import jax.numpy as jnp
from jax import lax
from jax.experimental import pallas as pl
from jax.experimental.pallas import tpu as pltpu
from jax.sharding import PartitionSpec as P

RANK = 64
TARGET_RANK = 128


def random_signs(seed_value, cell_index, column_index):
    hashed = cell_index * 73856093 + column_index * 19349663 + seed_value * 83492791
    hashed = jnp.bitwise_xor(hashed, lax.shift_right_logical(hashed, jnp.full_like(hashed, 15)))
    hashed = hashed * 668265261
    hashed = jnp.bitwise_xor(hashed, lax.shift_right_logical(hashed, jnp.full_like(hashed, 13)))
    parity = jnp.bitwise_and(
        lax.shift_right_logical(hashed, jnp.full_like(hashed, 7)), jnp.full_like(hashed, 1)
    )
    return jnp.where(parity == 1, 1.0, -1.0).astype(jnp.float32)


def body(thermal_field, generator_keys, slab_top_offset):
    exact_matmul_mode = lax.Precision.HIGHEST
    front_length, back_length, vertical_layer = thermal_field.shape
    devices_first = lax.axis_size("gx")
    devices_second = lax.axis_size("gy")
    total_first = front_length * devices_first
    total_second = back_length * devices_second
    x_index = (lax.axis_index("gx") * front_length + jnp.arange(front_length, dtype=jnp.int32))[
        :, None
    ]
    y_index = (lax.axis_index("gy") * back_length + jnp.arange(back_length, dtype=jnp.int32))[
        :, None
    ]
    z_index = (slab_top_offset[0] + jnp.arange(vertical_layer, dtype=jnp.int32))[:, None]
    rank_cols = jnp.arange(RANK, dtype=jnp.int32)[None, :]
    core_cols = jnp.arange(TARGET_RANK, dtype=jnp.int32)[None, :]
    omega_x = random_signs(generator_keys[0], x_index, rank_cols)
    omega_y = random_signs(generator_keys[1], y_index, rank_cols)
    omega_z = random_signs(generator_keys[2], z_index, rank_cols)
    phi_xt = random_signs(generator_keys[3], x_index, core_cols).T
    phi_yt = random_signs(generator_keys[4], y_index, core_cols).T
    phi_z = random_signs(generator_keys[5], z_index, core_cols)
    unrolled_grid = thermal_field.reshape(front_length * back_length, vertical_layer)
    reduced = jnp.dot(unrolled_grid, omega_z, precision=exact_matmul_mode).reshape(
        front_length, back_length, RANK
    )
    partial_x = jnp.einsum("xyk,yk->xk", reduced, omega_y, precision=exact_matmul_mode)
    partial_y = jnp.einsum("xyk,xk->yk", reduced, omega_x, precision=exact_matmul_mode)
    khatri = (omega_x[:, None, :] * omega_y[None, :, :]).reshape(front_length * back_length, RANK)
    partial_z = jnp.einsum("pz,pk->zk", unrolled_grid, khatri, precision=exact_matmul_mode)
    summed_x, half_z = lax.psum((partial_x, partial_z), "gy")
    summed_y, summed_z = lax.psum((partial_y, half_z), "gx")
    factor_x = summed_x * (1.0 / math.sqrt(total_second * vertical_layer))
    factor_y = summed_y * (1.0 / math.sqrt(total_first * vertical_layer))
    factor_z = summed_z * (1.0 / math.sqrt(total_first * total_second))
    thermal_matrix = thermal_field.reshape(front_length, back_length * vertical_layer)
    chosen_entries = phi_xt
    reduced_first = lax.psum_scatter(
        jnp.dot(chosen_entries, thermal_matrix, precision=exact_matmul_mode),
        "gx",
        scatter_dimension=0,
        tiled=True,
    )
    reduced_first = reduced_first.reshape(-1, back_length, vertical_layer)
    chosen_entries = phi_yt
    middle = jnp.einsum("by,ayz->baz", chosen_entries, reduced_first, precision=exact_matmul_mode)
    swapped = lax.psum_scatter(
        jnp.einsum("baz,zc->bac", middle, phi_z, precision=exact_matmul_mode),
        "gy",
        scatter_dimension=0,
        tiled=True,
    )
    core_block = jnp.transpose(swapped, (1, 0, 2))
    core = core_block * (1.0 / math.sqrt(total_first * total_second * vertical_layer))
    return (factor_x, factor_y, factor_z, core)


SUB = 8
LANES = 128
PARTS = 2
MESH_ID = pl.DeviceIdType.MESH


def signs(seed_value, cell_index, column_index):
    hashed = cell_index * 73856093 + column_index * 19349663 + seed_value * 83492791
    hashed = hashed ^ lax.shift_right_logical(hashed, jnp.full_like(hashed, 15))
    hashed = hashed * 668265261
    hashed = hashed ^ lax.shift_right_logical(hashed, jnp.full_like(hashed, 13))
    return jnp.where((hashed & 128) != 0, 1.0, -1.0).astype(jnp.float32)


def iota(shape, axis):
    return lax.broadcasted_iota(jnp.int32, shape, axis)


def split(value):
    high = value.astype(jnp.bfloat16)
    low = (value - high.astype(jnp.float32)).astype(jnp.bfloat16)
    return high, low


def mm(left, right):
    return jnp.dot(left, right, preferred_element_type=jnp.float32)


def flip(index, bit):
    return index + bit - 2 * bit * ((index // bit) % 2)


def way_of(group, groups, half):
    if 2 * group + 1 == groups:
        return half
    return 0 if 2 * group < groups else 1


def step_x(ix, way, turn):
    low = flip(ix, 1)
    high = flip(ix, 2)
    first = low + (high - low) * way
    return first if turn == 0 else low + high - first


def kernel(
    dims,
    keys_in, top, field_in,
    out_x, out_y, out_z, out_core,
    keys, field, load_sem, raw_out, raw_in, spread, landed, own, near, keep, edge_out, part_out, part_in,
    first_w, second_w, phi_y, phi_edge, phi_z,
    small_out, small_in, small_sum, zsum_in, zx_out, zx_in, fy_out, fy_in,
    s0, r0, s5, r5, s1, r1, s2, r2, s3, r3, s6, t1, u1, t2, u2, t3, u3, t4, u4,
):
    nx, ng, front, back, depth = dims
    nz = ng // 2
    blk_a = TARGET_RANK // nx
    pairs = blk_a // 2
    out_b = TARGET_RANK // ng
    ix = lax.axis_index("gx")
    ig = lax.axis_index("gy")
    iz, core = ig // 2, ig % 2
    inner = ((iz + 1) // 2) % 2

    def dev_x(d):
        r = ix
        for bit in (1, 2):
            if d & bit:
                r = flip(r, bit)
        return r

    def dev_g(d):
        r = ig
        for bit in (1, 2, 4):
            if d & bit:
                r = flip(r, bit)
        return r

    def copy(src, dst, send, recv, dx, dg):
        return pltpu.make_async_remote_copy(
            src_ref=src, dst_ref=dst, send_sem=send, recv_sem=recv,
            device_id=(dev_x(dx), dev_g(dg)), device_id_type=MESH_ID,
        )

    load = pltpu.make_async_copy(field_in, field, load_sem.at[0])
    load.start()
    load_keys = pltpu.make_async_copy(keys_in, keys, load_sem.at[1])
    load_keys.start()
    partners = [(dx, dc) for dx in range(nx) for dc in range(2) if dx or dc]
    partners += [(0, dg) for dg in range(2, ng)]
    barrier = pltpu.get_barrier_semaphore()
    for dx, dg in partners:
        pl.semaphore_signal(
            barrier, inc=1, device_id=(dev_x(dx), dev_g(dg)), device_id_type=MESH_ID
        )

    x0 = ix * front
    y0 = ig * back
    groups = back // SUB
    order = list(range(0, groups, 2)) + list(range(1, groups, 2))
    fold = front // 2
    deep = depth // 2
    two_d = field.reshape(front * back, depth)
    lower = iota((fold, SUB, depth), 2) < deep
    load.wait()
    for h in range(2):
        for g in order:
            here = field[0:fold, g * SUB : (g + 1) * SUB, :]
            there = field[fold:front, g * SUB : (g + 1) * SUB, :]
            if h == 0:
                raw_out[h, g] = jnp.where(lower, here, pltpu.roll(there, deep, 2))
            else:
                raw_out[h, g] = jnp.where(lower, pltpu.roll(here, deep, 2), there)
    pl.semaphore_wait(barrier, len(partners))
    raws = {}
    for h in range(2):
        for g in order:
            raws[h, g] = pltpu.make_async_remote_copy(
                src_ref=raw_out.at[h, g], dst_ref=raw_in.at[h, g],
                send_sem=s0.at[h, g], recv_sem=r0.at[h, g],
                device_id=(step_x(ix, way_of(g, groups, h), 0), ig), device_id_type=MESH_ID,
            )
            raws[h, g].start()
    pend = list(raws.values())
    load_keys.wait()
    z0 = top[0]

    lane = iota((RANK, 2 * front), 1)
    left = signs(
        keys[0], jnp.where(lane >= front, lane - front, lane) + x0, iota((RANK, 2 * front), 0)
    ).astype(jnp.bfloat16)
    omega_yt = signs(keys[1], iota((RANK, back), 1) + y0, iota((RANK, back), 0))
    total_z = jnp.zeros((RANK, depth), jnp.float32)
    for y in range(back):
        high, low = split(two_d[pl.ds(y, front, stride=back), :])
        both = mm(left, jnp.concatenate([high, low], axis=0))
        total_z = total_z + both * omega_yt[:, y : y + 1]

    lane_z = iota((depth, LANES), 1)
    row_z = iota((depth, LANES), 0) + z0
    omega_z = signs(keys[2], row_z, lane_z).astype(jnp.bfloat16)
    high, low = split(two_d[...])
    reduced = (mm(high, omega_z) + mm(low, omega_z)).reshape(front, back, LANES)
    omega_y = signs(keys[1], iota((back, LANES), 0) + y0, iota((back, LANES), 1))
    part_y = jnp.zeros((back, LANES), jnp.float32)
    omega_x = signs(keys[0], iota((front, LANES), 0) + x0, iota((front, LANES), 1))
    part_x = jnp.sum(reduced * omega_y[None], axis=1)
    for x in range(front):
        part_y = part_y + reduced[x] * omega_x[x : x + 1]
    fy_out[...] = part_y
    per = front // ng
    kper = RANK // ng
    for d in range(ng):
        small_out[d, 0:kper] = total_z[d * kper : (d + 1) * kper]
        small_out[d, SUB : SUB + per] = part_x[d * per : (d + 1) * per]
    sm = []
    for d in range(1, ng):
        sm.append(copy(
            small_out.at[dev_g(d)], small_in.at[d - 1], t2.at[d - 1], u2.at[d - 1], 0, d
        ))
        sm[-1].start()

    def weights(base, far_x):
        shape = (4 * pairs, 4 * fold)
        row = iota(shape, 0)
        lane = iota(shape, 1)
        lane = jnp.where(lane >= front, lane - front, lane)
        second = row >= 2 * pairs
        row = jnp.where(second, row - 2 * pairs, row)
        swapped = jnp.where(lane >= fold, lane - fold, lane + fold)
        cell = jnp.where(second, swapped, lane) + base
        target = jnp.where(row < pairs, ix * blk_a, far_x * blk_a - pairs) + row
        target = jnp.where(second, target + pairs, target)
        return signs(keys[3], cell, target).astype(jnp.bfloat16)

    for way in range(2):
        first_w[way] = weights(x0, step_x(ix, way, 1))
        second_w[way] = weights(step_x(ix, way, 0) * front, step_x(ix, way, 1))

    lower_row = iota((2 * pairs, depth), 1) < deep

    def contract(left, packed):
        both = jnp.concatenate([packed, pltpu.roll(packed, deep, 1)], axis=0)
        high, low = split(both)
        out = mm(left, jnp.concatenate([high, low], axis=0))
        return jnp.where(lower_row, out[: 2 * pairs], out[2 * pairs :])

    for h in range(2):
        wide = spread.at[h].reshape(2 * pairs * back, depth)
        for g in order:
            flat = raw_out.at[h, g].reshape(fold * SUB, depth)
            for y in range(SUB):
                wide[pl.ds(g * SUB + y, 2 * pairs, stride=back), :] = contract(
                    first_w[way_of(g, groups, h)], flat[pl.ds(y, fold, stride=SUB), :]
                )

    shape = (6 * out_b, 4 * back)
    row = iota(shape, 0)
    col = iota(shape, 1)
    col = jnp.where(col >= 2 * back, col - 2 * back, col)
    target = row
    for k, d in enumerate((4, 5, 6, 7, 0, 1)):
        target = jnp.where(row >= k * out_b, row + (dev_g(d) - k) * out_b, target)
    for src in range(2):
        cell = jnp.where(col >= back, dev_g(2 * src + 1) * back - back, dev_g(2 * src) * back) + col
        phi_y[:, src * 4 * back : (src + 1) * 4 * back] = signs(keys[4], cell, target).astype(
            jnp.bfloat16
        )
        if src == 0:
            row = row[: 2 * out_b]
            here = ig + (dev_g(2) - ig) * inner
            there = dev_g(1) + (dev_g(3) - dev_g(1)) * inner
            target_edge = row + jnp.where(row >= out_b, there - 1, here) * out_b
            phi_edge[...] = signs(keys[4], cell[: 2 * out_b], target_edge).astype(jnp.bfloat16)

    @pl.when(inner == 1)
    def _():
        for h in range(2):
            part_in[h, :, 3:5] = jnp.zeros((PARTS, 2, SUB // PARTS, out_b, depth), jnp.float32)

    row = iota((depth, 2 * LANES), 0)
    col = iota((depth, 2 * LANES), 1)
    same = (row >= deep) == (col >= LANES)
    row = jnp.where(row >= deep, row - deep, row) + z0
    col = jnp.where(col >= LANES, col - LANES, col)
    for h in range(2):
        phi_z[h] = jnp.where(same, signs(keys[5], row + h * deep, col), 0.0).astype(jnp.bfloat16)

    rows = SUB // PARTS
    zx = []

    def sum_small():
        for c in sm:
            c.wait_recv()
        block = small_out[ig]
        for d in range(1, ng):
            block = block + small_in[d - 1]
        small_sum[...] = block
        for d in range(1, nx):
            zx.append(copy(
                small_sum.at[0:SUB], zsum_in.at[d - 1], t3.at[d - 1], u3.at[d - 1], d, 0
            ))
            zx[-1].start()

    def receive_raw(h):
        wide = spread.at[h].reshape(2 * pairs * back, depth)
        sends = [[] for _ in range(PARTS)]
        for g in order:
            raws[h, g].wait_recv()
            flat = raw_in.at[h, g].reshape(fold * SUB, depth)
            for y in range(SUB):
                strip = pl.ds(g * SUB + y, 2 * pairs, stride=back)
                wide[strip, :] = wide[strip, :] + contract(
                    second_w[way_of(g, groups, h)], flat[pl.ds(y, fold, stride=SUB), :]
                )
            for p in range(PARTS):
                for dc in (1, 0):
                    start = pairs + (dev_g(dc) % 2) * SUB + p * rows
                    ys = slice(g * SUB, (g + 1) * SUB)
                    sends[p].append(pltpu.make_async_remote_copy(
                        src_ref=spread.at[h, pl.ds(start, rows), ys, :],
                        dst_ref=landed.at[h, dc, p * rows : (p + 1) * rows, ys, :],
                        send_sem=s1.at[h, p, dc, g], recv_sem=r1.at[h, p, dc, g],
                        device_id=(step_x(ix, way_of(g, groups, h), 1), dev_g(dc)),
                        device_id_type=MESH_ID,
                    ))
                    sends[p][-1].start()
        for p in range(PARTS):
            sends[p].append(copy(
                spread.at[h, pl.ds((1 - core) * SUB + p * rows, rows)],
                landed.at[h, 2, p * rows : (p + 1) * rows],
                s5.at[h, p], r5.at[h, p], 0, 1,
            ))
            sends[p][-1].start()
        return sends

    nearby = {}
    edges = {}
    share = {}

    def send_near(h, p, sends):
        for c in sends[p]:
            c.wait_recv()
        at = slice(p * rows, (p + 1) * rows)
        own[h, at, 0] = spread[h, pl.ds(core * SUB + p * rows, rows)] + landed[h, 0, at]
        own[h, at, 1] = landed[h, 2, at] + landed[h, 1, at]
        nearby[h, p] = copy(own.at[h, at], near.at[h, at], s2.at[h, p], r2.at[h, p], 0, 2)

        @pl.when(inner == 0)
        def _():
            nearby[h, p].start()

        for r in range(rows):
            pieces = split(own[h, p * rows + r].reshape(2 * back, depth))
            total = mm(phi_edge[...], jnp.concatenate(pieces, axis=0))
            edge_out[h, p, 0, r] = total[:out_b]
            edge_out[h, p, 1, r] = total[out_b:]
        for k in range(2):
            edges[h, p, k] = copy(
                edge_out.at[h, p, k], part_in.at[h, p, 3 + k],
                s3.at[h, p, 3 + k], r3.at[h, p, 3 + k], 0, 2 + k,
            )
        share[h, p, 0] = copy(
            edge_out.at[h, p, 1], part_in.at[h, p, 0], s3.at[h, p, 0], r3.at[h, p, 0], 0, 1
        )

        @pl.when(inner == 1)
        def _():
            edges[h, p, 0].start()
            edges[h, p, 1].start()

        @pl.when(inner == 0)
        def _():
            keep[h, at] = edge_out[h, p, 0]
            share[h, p, 0].start()


    first = receive_raw(0)
    sum_small()
    second = receive_raw(1)
    fy = []
    for d in range(1, nx):
        fy.append(copy(fy_out, fy_in.at[d - 1], t1.at[d - 1], u1.at[d - 1], d, 0))
        fy[-1].start()
    pend += fy
    send_near(0, 0, first)
    send_near(0, 1, first)
    for c in zx:
        c.wait_recv()
    zpart = small_sum[0:SUB]
    for d in range(1, nx):
        zpart = zpart + zsum_in[d - 1]
    zx_out[0:SUB] = zpart
    zx_out[SUB:] = small_sum[SUB:]
    gathered = []
    for d in range(1, ng):
        gathered.append(copy(zx_out, zx_in.at[d - 1], t4.at[d - 1], u4.at[d - 1], 0, d))
        gathered[-1].start()
    send_near(1, 0, second)
    send_near(1, 1, second)
    pend += sum(first + second, []) + zx + gathered

    parts = {}
    ways = ((0, 4, 1), (1, 5, 2), (2, 6, 1), (3, 7, 2), (4, 1, 0))
    for h in range(2):
        for p in range(PARTS):
            for k, d, slot in ways:
                parts[h, p, k] = copy(
                    part_out.at[h, p, k], part_in.at[h, p, slot],
                    s6.at[h, p, k], r3.at[h, p, slot], 0, d,
                )

    @pl.when(inner == 1)
    def _():
        for h in range(2):
            for p in range(PARTS):
                nearby[h, p].wait_recv()
                for r in range(rows):
                    at = p * rows + r
                    pieces = split(own[h, at].reshape(2 * back, depth))
                    pieces += split(near[h, at].reshape(2 * back, depth))
                    total = mm(phi_y[...], jnp.concatenate(pieces, axis=0))
                    keep[h, at] = total[4 * out_b : 5 * out_b]
                    for k in range(5):
                        first = (k if k < 4 else 5) * out_b
                        part_out[h, p, k, r] = total[first : first + out_b]
                for k in range(5):
                    parts[h, p, k].start()

    for c in fy:
        c.wait_recv()
    value = fy_out[...]
    for d in range(1, nx):
        value = value + fy_in[d - 1]
    out_y[...] = (value * (1.0 / math.sqrt(front * nx * depth)))[:, :RANK]
    for c in gathered:
        c.wait_recv()
    for c in sm:
        c.wait_send()
    for d in range(ng):
        block = zx_out[...] if d == 0 else zx_in[d - 1]
        small_out[dev_g(d)] = block
    scale_x = 1.0 / math.sqrt(back * ng * depth)
    scale_z = 1.0 / math.sqrt(front * nx * back * ng)
    for d in range(ng):
        out_x[d * per : (d + 1) * per, :] = small_out[d, SUB : SUB + per, :RANK] * scale_x
        out_z[d * kper : (d + 1) * kper, :] = small_out[d, 0:kper] * scale_z

    scale = 1.0 / math.sqrt(front * nx * back * ng * depth)
    count = rows * out_b
    for h in range(2):
        for p in range(PARTS):
            @pl.when(inner == 0)
            def _():
                edges[h, p, 0].wait_recv()
                edges[h, p, 1].wait_recv()

            share[h, p, 0].wait_recv()
            parts[h, p, 0].wait_recv()
            parts[h, p, 1].wait_recv()
            at = slice(p * rows, (p + 1) * rows)
            mine = keep[h, at] + part_in[h, p, 3] + part_in[h, p, 1]
            other = part_in[h, p, 0] + part_in[h, p, 4] + part_in[h, p, 2]
            mine = mine.reshape(count, depth)
            other = other.reshape(count, depth)
            high, low = split(jnp.concatenate([mine, other], axis=0))
            value = (mm(high, phi_z[h]) + mm(low, phi_z[h])) * scale
            for i in range(2):
                for which in range(2):
                    side = core if which == 0 else 1 - core
                    start = pl.multiple_of((i * pairs + side * SUB + p * rows) * out_b, SUB)
                    place = pl.ds(start, count)
                    piece = value[which * count : (which + 1) * count, i * LANES : (i + 1) * LANES]
                    out_core[place, :] = piece if h == 0 else out_core[place, :] + piece
    for c in pend:
        c.wait_send()

    @pl.when(inner == 0)
    def _():
        for c in list(nearby.values()) + list(share.values()):
            c.wait_send()

    @pl.when(inner == 1)
    def _():
        for c in list(edges.values()) + list(parts.values()):
            c.wait_send()


def publish(*refs):
    ready, out, sems = refs[:4], refs[4:8], refs[8]
    copies = [pltpu.make_async_copy(a, b, sems.at[i]) for i, (a, b) in enumerate(zip(ready, out))]
    for c in copies:
        c.start()
    for c in copies:
        c.wait()


def fused_body(nx, ng, thermal_field, generator_keys, slab_top_offset):
    front, back, depth = thermal_field.shape
    blk_a = TARGET_RANK // nx
    out_b = TARGET_RANK // ng
    f32 = jnp.float32
    bf16 = jnp.bfloat16
    vmem = pltpu.VMEM
    dma = pltpu.SemaphoreType.DMA
    groups = back // SUB
    rows = SUB // PARTS
    scratch = [
        pltpu.SMEM(generator_keys.shape, jnp.int32),
        vmem((front, back, depth), f32),
        dma((2,)),
        vmem((2, groups, front // 2, SUB, depth), f32),
        vmem((2, groups, front // 2, SUB, depth), f32),
        vmem((2, blk_a, back, depth), f32),
        vmem((2, 3, SUB, back, depth), f32),
        vmem((2, SUB, 2, back, depth), f32),
        vmem((2, SUB, 2, back, depth), f32),
        vmem((2, SUB, out_b, depth), f32),
        vmem((2, PARTS, 2, rows, out_b, depth), f32),
        vmem((2, PARTS, 5, rows, out_b, depth), f32),
        vmem((2, PARTS, 5, rows, out_b, depth), f32),
        vmem((2, 2 * blk_a, 2 * front), bf16),
        vmem((2, 2 * blk_a, 2 * front), bf16),
        vmem((6 * out_b, 8 * back), bf16),
        vmem((2 * out_b, 4 * back), bf16),
        vmem((2, depth, 2 * LANES), bf16),
        vmem((ng, 2 * SUB, LANES), f32),
        vmem((ng - 1, 2 * SUB, LANES), f32),
        vmem((2 * SUB, LANES), f32),
        vmem((nx - 1, SUB, LANES), f32),
        vmem((2 * SUB, LANES), f32),
        vmem((ng - 1, 2 * SUB, LANES), f32),
        vmem((back, LANES), f32),
        vmem((nx - 1, back, LANES), f32),
        dma((2, groups)), dma((2, groups)),
        dma((2, PARTS)), dma((2, PARTS)),
        dma((2, PARTS, 2, groups)), dma((2, PARTS, 2, groups)),
        dma((2, PARTS)), dma((2, PARTS)),
        dma((2, PARTS, 5)), dma((2, PARTS, 5)), dma((2, PARTS, 5)),
        dma((nx - 1,)), dma((nx - 1,)),
        dma((ng - 1,)), dma((ng - 1,)),
        dma((nx - 1,)), dma((nx - 1,)),
        dma((ng - 1,)), dma((ng - 1,)),
    ]
    whole = pl.BlockSpec(memory_space=pltpu.VMEM)
    far = pl.BlockSpec(memory_space=pltpu.HBM)
    shapes = (
        jax.ShapeDtypeStruct((front, RANK), f32),
        jax.ShapeDtypeStruct((back, RANK), f32),
        jax.ShapeDtypeStruct((RANK, depth), f32),
        jax.ShapeDtypeStruct((blk_a * out_b, depth), f32),
    )
    def stay(array):
        return pltpu.with_memory_space_constraint(array, pltpu.HBM)

    results = pl.pallas_call(
        functools.partial(kernel, (nx, ng, front, back, depth)),
        out_shape=shapes,
        in_specs=[far, pl.BlockSpec(memory_space=pltpu.SMEM), far],
        out_specs=(whole,) * 4,
        scratch_shapes=scratch,
        compiler_params=pltpu.CompilerParams(
            collective_id=0, has_side_effects=True, vmem_limit_bytes=40 * 2**20
        ),
    )(stay(generator_keys), slab_top_offset, stay(thermal_field))
    fx, fy, fz, core = pl.pallas_call(
        publish,
        out_shape=shapes,
        in_specs=[whole] * 4,
        out_specs=(far,) * 4,
        scratch_shapes=[dma((4,))],
        compiler_params=pltpu.CompilerParams(vmem_limit_bytes=2**20),
    )(*results)
    return fx, fy, fz.T, core.reshape(blk_a, out_b, depth)


def suits(nx, ng):
    return nx == 4 and ng == 8


def solution(mesh):
    nx, ng = mesh.shape["gx"], mesh.shape["gy"]
    chosen = functools.partial(fused_body, nx, ng) if suits(nx, ng) else body
    placed = (P("gx", "gy", None), P(), P())
    return jax.shard_map(
        chosen,
        mesh=mesh,
        in_specs=placed,
        out_specs=(P("gx", None), P("gy", None), P(), P("gx", "gy", None)),
        check_vma=False,
    )
```

```python
import functools
import math

import jax
import jax.numpy as jnp
from jax import lax
from jax.experimental import pallas as pl
from jax.experimental.pallas import tpu as pltpu
from jax.sharding import PartitionSpec as P

RANK = 64
TARGET_RANK = 128


def random_signs(seed_value, cell_index, column_index):
    hashed = cell_index * 73856093 + column_index * 19349663 + seed_value * 83492791
    hashed = jnp.bitwise_xor(hashed, lax.shift_right_logical(hashed, jnp.full_like(hashed, 15)))
    hashed = hashed * 668265261
    hashed = jnp.bitwise_xor(hashed, lax.shift_right_logical(hashed, jnp.full_like(hashed, 13)))
    parity = jnp.bitwise_and(
        lax.shift_right_logical(hashed, jnp.full_like(hashed, 7)), jnp.full_like(hashed, 1)
    )
    return jnp.where(parity == 1, 1.0, -1.0).astype(jnp.float32)


def body(thermal_field, generator_keys, slab_top_offset):
    exact_matmul_mode = lax.Precision.HIGHEST
    front_length, back_length, vertical_layer = thermal_field.shape
    devices_first = lax.axis_size("gx")
    devices_second = lax.axis_size("gy")
    total_first = front_length * devices_first
    total_second = back_length * devices_second
    x_index = (lax.axis_index("gx") * front_length + jnp.arange(front_length, dtype=jnp.int32))[
        :, None
    ]
    y_index = (lax.axis_index("gy") * back_length + jnp.arange(back_length, dtype=jnp.int32))[
        :, None
    ]
    z_index = (slab_top_offset[0] + jnp.arange(vertical_layer, dtype=jnp.int32))[:, None]
    rank_cols = jnp.arange(RANK, dtype=jnp.int32)[None, :]
    core_cols = jnp.arange(TARGET_RANK, dtype=jnp.int32)[None, :]
    omega_x = random_signs(generator_keys[0], x_index, rank_cols)
    omega_y = random_signs(generator_keys[1], y_index, rank_cols)
    omega_z = random_signs(generator_keys[2], z_index, rank_cols)
    phi_xt = random_signs(generator_keys[3], x_index, core_cols).T
    phi_yt = random_signs(generator_keys[4], y_index, core_cols).T
    phi_z = random_signs(generator_keys[5], z_index, core_cols)
    unrolled_grid = thermal_field.reshape(front_length * back_length, vertical_layer)
    reduced = jnp.dot(unrolled_grid, omega_z, precision=exact_matmul_mode).reshape(
        front_length, back_length, RANK
    )
    partial_x = jnp.einsum("xyk,yk->xk", reduced, omega_y, precision=exact_matmul_mode)
    partial_y = jnp.einsum("xyk,xk->yk", reduced, omega_x, precision=exact_matmul_mode)
    khatri = (omega_x[:, None, :] * omega_y[None, :, :]).reshape(front_length * back_length, RANK)
    partial_z = jnp.einsum("pz,pk->zk", unrolled_grid, khatri, precision=exact_matmul_mode)
    summed_x, half_z = lax.psum((partial_x, partial_z), "gy")
    summed_y, summed_z = lax.psum((partial_y, half_z), "gx")
    factor_x = summed_x * (1.0 / math.sqrt(total_second * vertical_layer))
    factor_y = summed_y * (1.0 / math.sqrt(total_first * vertical_layer))
    factor_z = summed_z * (1.0 / math.sqrt(total_first * total_second))
    thermal_matrix = thermal_field.reshape(front_length, back_length * vertical_layer)
    chosen_entries = phi_xt
    reduced_first = lax.psum_scatter(
        jnp.dot(chosen_entries, thermal_matrix, precision=exact_matmul_mode),
        "gx",
        scatter_dimension=0,
        tiled=True,
    )
    reduced_first = reduced_first.reshape(-1, back_length, vertical_layer)
    chosen_entries = phi_yt
    middle = jnp.einsum("by,ayz->baz", chosen_entries, reduced_first, precision=exact_matmul_mode)
    swapped = lax.psum_scatter(
        jnp.einsum("baz,zc->bac", middle, phi_z, precision=exact_matmul_mode),
        "gy",
        scatter_dimension=0,
        tiled=True,
    )
    core_block = jnp.transpose(swapped, (1, 0, 2))
    core = core_block * (1.0 / math.sqrt(total_first * total_second * vertical_layer))
    return (factor_x, factor_y, factor_z, core)


SUB = 8
LANES = 128
PARTS = 2
MESH_ID = pl.DeviceIdType.MESH


def signs(seed_value, cell_index, column_index):
    hashed = cell_index * 73856093 + column_index * 19349663 + seed_value * 83492791
    hashed = hashed ^ lax.shift_right_logical(hashed, jnp.full_like(hashed, 15))
    hashed = hashed * 668265261
    hashed = hashed ^ lax.shift_right_logical(hashed, jnp.full_like(hashed, 13))
    return jnp.where((hashed & 128) != 0, 1.0, -1.0).astype(jnp.float32)


def iota(shape, axis):
    return lax.broadcasted_iota(jnp.int32, shape, axis)


def split(value):
    high = value.astype(jnp.bfloat16)
    low = (value - high.astype(jnp.float32)).astype(jnp.bfloat16)
    return high, low


def mm(left, right):
    return jnp.dot(left, right, preferred_element_type=jnp.float32)


def flip(index, bit):
    return index + bit - 2 * bit * ((index // bit) % 2)


def way_of(group, groups, half):
    if 2 * group + 1 == groups:
        return half
    return 0 if 2 * group < groups else 1


def step_x(ix, way, turn):
    low = flip(ix, 1)
    high = flip(ix, 2)
    first = low + (high - low) * way
    return first if turn == 0 else low + high - first


def kernel(
    dims,
    keys_in, top, field_in,
    out_x, out_y, out_z, out_core,
    keys, field, load_sem, raw_out, raw_in, spread, landed, own, near, keep, edge_out, part_out, part_in,
    first_w, second_w, phi_y, phi_edge, phi_z,
    small_out, small_in, small_sum, zsum_in, zx_out, zx_in, fy_out, fy_in,
    s0, r0, s5, r5, s1, r1, s2, r2, s3, r3, s6, t1, u1, t2, u2, t3, u3, t4, u4,
):
    nx, ng, front, back, depth = dims
    nz = ng // 2
    blk_a = TARGET_RANK // nx
    pairs = blk_a // 2
    out_b = TARGET_RANK // ng
    ix = lax.axis_index("gx")
    ig = lax.axis_index("gy")
    iz, core = ig // 2, ig % 2
    inner = ((iz + 1) // 2) % 2

    def dev_x(d):
        r = ix
        for bit in (1, 2):
            if d & bit:
                r = flip(r, bit)
        return r

    def dev_g(d):
        r = ig
        for bit in (1, 2, 4):
            if d & bit:
                r = flip(r, bit)
        return r

    def copy(src, dst, send, recv, dx, dg):
        return pltpu.make_async_remote_copy(
            src_ref=src, dst_ref=dst, send_sem=send, recv_sem=recv,
            device_id=(dev_x(dx), dev_g(dg)), device_id_type=MESH_ID,
        )

    load = pltpu.make_async_copy(field_in, field, load_sem.at[0])
    load.start()
    load_keys = pltpu.make_async_copy(keys_in, keys, load_sem.at[1])
    load_keys.start()
    partners = [(dx, dc) for dx in range(nx) for dc in range(2) if dx or dc]
    partners += [(0, dg) for dg in range(2, ng)]
    barrier = pltpu.get_barrier_semaphore()
    for dx, dg in partners:
        pl.semaphore_signal(
            barrier, inc=1, device_id=(dev_x(dx), dev_g(dg)), device_id_type=MESH_ID
        )

    x0 = ix * front
    y0 = ig * back
    groups = back // SUB
    order = list(range(0, groups, 2)) + list(range(1, groups, 2))
    fold = front // 2
    deep = depth // 2
    two_d = field.reshape(front * back, depth)
    lower = iota((fold, SUB, depth), 2) < deep
    load.wait()
    for h in range(2):
        for g in order:
            here = field[0:fold, g * SUB : (g + 1) * SUB, :]
            there = field[fold:front, g * SUB : (g + 1) * SUB, :]
            if h == 0:
                raw_out[h, g] = jnp.where(lower, here, pltpu.roll(there, deep, 2))
            else:
                raw_out[h, g] = jnp.where(lower, pltpu.roll(here, deep, 2), there)
    pl.semaphore_wait(barrier, len(partners))
    raws = {}
    for h in range(2):
        for g in order:
            raws[h, g] = pltpu.make_async_remote_copy(
                src_ref=raw_out.at[h, g], dst_ref=raw_in.at[h, g],
                send_sem=s0.at[h, g], recv_sem=r0.at[h, g],
                device_id=(step_x(ix, way_of(g, groups, h), 0), ig), device_id_type=MESH_ID,
            )
            raws[h, g].start()
    pend = list(raws.values())
    load_keys.wait()
    z0 = top[0]

    lane = iota((RANK, 2 * front), 1)
    left = signs(
        keys[0], jnp.where(lane >= front, lane - front, lane) + x0, iota((RANK, 2 * front), 0)
    ).astype(jnp.bfloat16)
    omega_yt = signs(keys[1], iota((RANK, back), 1) + y0, iota((RANK, back), 0))
    total_z = jnp.zeros((RANK, depth), jnp.float32)
    for y in range(back):
        high, low = split(two_d[pl.ds(y, front, stride=back), :])
        both = mm(left, jnp.concatenate([high, low], axis=0))
        total_z = total_z + both * omega_yt[:, y : y + 1]

    lane_z = iota((depth, LANES), 1)
    row_z = iota((depth, LANES), 0) + z0
    omega_z = signs(keys[2], row_z, lane_z).astype(jnp.bfloat16)
    high, low = split(two_d[...])
    reduced = (mm(high, omega_z) + mm(low, omega_z)).reshape(front, back, LANES)
    omega_y = signs(keys[1], iota((back, LANES), 0) + y0, iota((back, LANES), 1))
    part_y = jnp.zeros((back, LANES), jnp.float32)
    omega_x = signs(keys[0], iota((front, LANES), 0) + x0, iota((front, LANES), 1))
    part_x = jnp.sum(reduced * omega_y[None], axis=1)
    for x in range(front):
        part_y = part_y + reduced[x] * omega_x[x : x + 1]
    fy_out[...] = part_y
    per = front // ng
    kper = RANK // ng
    for d in range(ng):
        small_out[d, 0:kper] = total_z[d * kper : (d + 1) * kper]
        small_out[d, SUB : SUB + per] = part_x[d * per : (d + 1) * per]
    sm = []
    for d in range(1, ng):
        sm.append(copy(
            small_out.at[dev_g(d)], small_in.at[d - 1], t2.at[d - 1], u2.at[d - 1], 0, d
        ))
        sm[-1].start()

    def weights(base, far_x):
        shape = (4 * pairs, 4 * fold)
        row = iota(shape, 0)
        lane = iota(shape, 1)
        lane = jnp.where(lane >= front, lane - front, lane)
        second = row >= 2 * pairs
        row = jnp.where(second, row - 2 * pairs, row)
        swapped = jnp.where(lane >= fold, lane - fold, lane + fold)
        cell = jnp.where(second, swapped, lane) + base
        target = jnp.where(row < pairs, ix * blk_a, far_x * blk_a - pairs) + row
        target = jnp.where(second, target + pairs, target)
        return signs(keys[3], cell, target).astype(jnp.bfloat16)

    for way in range(2):
        first_w[way] = weights(x0, step_x(ix, way, 1))
        second_w[way] = weights(step_x(ix, way, 0) * front, step_x(ix, way, 1))

    lower_row = iota((2 * pairs, depth), 1) < deep

    def contract(left, packed):
        both = jnp.concatenate([packed, pltpu.roll(packed, deep, 1)], axis=0)
        high, low = split(both)
        out = mm(left, jnp.concatenate([high, low], axis=0))
        return jnp.where(lower_row, out[: 2 * pairs], out[2 * pairs :])

    for h in range(2):
        wide = spread.at[h].reshape(2 * pairs * back, depth)
        for g in order:
            flat = raw_out.at[h, g].reshape(fold * SUB, depth)
            for y in range(SUB):
                wide[pl.ds(g * SUB + y, 2 * pairs, stride=back), :] = contract(
                    first_w[way_of(g, groups, h)], flat[pl.ds(y, fold, stride=SUB), :]
                )

    shape = (6 * out_b, 4 * back)
    row = iota(shape, 0)
    col = iota(shape, 1)
    col = jnp.where(col >= 2 * back, col - 2 * back, col)
    target = row
    for k, d in enumerate((4, 5, 6, 7, 0, 1)):
        target = jnp.where(row >= k * out_b, row + (dev_g(d) - k) * out_b, target)
    for src in range(2):
        cell = jnp.where(col >= back, dev_g(2 * src + 1) * back - back, dev_g(2 * src) * back) + col
        phi_y[:, src * 4 * back : (src + 1) * 4 * back] = signs(keys[4], cell, target).astype(
            jnp.bfloat16
        )
        if src == 0:
            row = row[: 2 * out_b]
            here = ig + (dev_g(2) - ig) * inner
            there = dev_g(1) + (dev_g(3) - dev_g(1)) * inner
            target_edge = row + jnp.where(row >= out_b, there - 1, here) * out_b
            phi_edge[...] = signs(keys[4], cell[: 2 * out_b], target_edge).astype(jnp.bfloat16)

    @pl.when(inner == 1)
    def _():
        for h in range(2):
            part_in[h, :, 3:5] = jnp.zeros((PARTS, 2, SUB // PARTS, out_b, depth), jnp.float32)

    row = iota((depth, 2 * LANES), 0)
    col = iota((depth, 2 * LANES), 1)
    same = (row >= deep) == (col >= LANES)
    row = jnp.where(row >= deep, row - deep, row) + z0
    col = jnp.where(col >= LANES, col - LANES, col)
    for h in range(2):
        phi_z[h] = jnp.where(same, signs(keys[5], row + h * deep, col), 0.0).astype(jnp.bfloat16)

    rows = SUB // PARTS
    zx = []

    def sum_small():
        for c in sm:
            c.wait_recv()
        block = small_out[ig]
        for d in range(1, ng):
            block = block + small_in[d - 1]
        small_sum[...] = block
        for d in range(1, nx):
            zx.append(copy(
                small_sum.at[0:SUB], zsum_in.at[d - 1], t3.at[d - 1], u3.at[d - 1], d, 0
            ))
            zx[-1].start()

    def receive_raw(h):
        wide = spread.at[h].reshape(2 * pairs * back, depth)
        sends = [[] for _ in range(PARTS)]
        for g in order:
            raws[h, g].wait_recv()
            flat = raw_in.at[h, g].reshape(fold * SUB, depth)
            for y in range(SUB):
                strip = pl.ds(g * SUB + y, 2 * pairs, stride=back)
                wide[strip, :] = wide[strip, :] + contract(
                    second_w[way_of(g, groups, h)], flat[pl.ds(y, fold, stride=SUB), :]
                )
            for p in range(PARTS):
                for dc in (1, 0):
                    start = pairs + (dev_g(dc) % 2) * SUB + p * rows
                    ys = slice(g * SUB, (g + 1) * SUB)
                    sends[p].append(pltpu.make_async_remote_copy(
                        src_ref=spread.at[h, pl.ds(start, rows), ys, :],
                        dst_ref=landed.at[h, dc, p * rows : (p + 1) * rows, ys, :],
                        send_sem=s1.at[h, p, dc, g], recv_sem=r1.at[h, p, dc, g],
                        device_id=(step_x(ix, way_of(g, groups, h), 1), dev_g(dc)),
                        device_id_type=MESH_ID,
                    ))
                    sends[p][-1].start()
        for p in range(PARTS):
            sends[p].append(copy(
                spread.at[h, pl.ds((1 - core) * SUB + p * rows, rows)],
                landed.at[h, 2, p * rows : (p + 1) * rows],
                s5.at[h, p], r5.at[h, p], 0, 1,
            ))
            sends[p][-1].start()
        return sends

    nearby = {}
    edges = {}
    share = {}

    def send_near(h, p, sends):
        for c in sends[p]:
            c.wait_recv()
        at = slice(p * rows, (p + 1) * rows)
        own[h, at, 0] = spread[h, pl.ds(core * SUB + p * rows, rows)] + landed[h, 0, at]
        own[h, at, 1] = landed[h, 2, at] + landed[h, 1, at]
        nearby[h, p] = copy(own.at[h, at], near.at[h, at], s2.at[h, p], r2.at[h, p], 0, 2)

        @pl.when(inner == 0)
        def _():
            nearby[h, p].start()

    def send_edges(h, p):
        at = slice(p * rows, (p + 1) * rows)
        for r in range(rows):
            pieces = split(own[h, p * rows + r].reshape(2 * back, depth))
            total = mm(phi_edge[...], jnp.concatenate(pieces, axis=0))
            edge_out[h, p, 0, r] = total[:out_b]
            edge_out[h, p, 1, r] = total[out_b:]
        for k in range(2):
            edges[h, p, k] = copy(
                edge_out.at[h, p, k], part_in.at[h, p, 3 + k],
                s3.at[h, p, 3 + k], r3.at[h, p, 3 + k], 0, 2 + k,
            )
        share[h, p, 0] = copy(
            edge_out.at[h, p, 1], part_in.at[h, p, 0], s3.at[h, p, 0], r3.at[h, p, 0], 0, 1
        )

        @pl.when(inner == 1)
        def _():
            edges[h, p, 0].start()
            edges[h, p, 1].start()

        @pl.when(inner == 0)
        def _():
            keep[h, at] = edge_out[h, p, 0]
            share[h, p, 0].start()


    first = receive_raw(0)
    sum_small()
    second = receive_raw(1)
    fy = []
    for d in range(1, nx):
        fy.append(copy(fy_out, fy_in.at[d - 1], t1.at[d - 1], u1.at[d - 1], d, 0))
        fy[-1].start()
    pend += fy
    for p in range(PARTS):
        send_near(0, p, first)
    for p in range(PARTS):
        send_edges(0, p)
    for c in zx:
        c.wait_recv()
    zpart = small_sum[0:SUB]
    for d in range(1, nx):
        zpart = zpart + zsum_in[d - 1]
    zx_out[0:SUB] = zpart
    zx_out[SUB:] = small_sum[SUB:]
    gathered = []
    for d in range(1, ng):
        gathered.append(copy(zx_out, zx_in.at[d - 1], t4.at[d - 1], u4.at[d - 1], 0, d))
        gathered[-1].start()
    for p in range(PARTS):
        send_near(1, p, second)
    for p in range(PARTS):
        send_edges(1, p)
    pend += sum(first + second, []) + zx + gathered

    parts = {}
    ways = ((0, 4, 1), (1, 5, 2), (2, 6, 1), (3, 7, 2), (4, 1, 0))
    for h in range(2):
        for p in range(PARTS):
            for k, d, slot in ways:
                parts[h, p, k] = copy(
                    part_out.at[h, p, k], part_in.at[h, p, slot],
                    s6.at[h, p, k], r3.at[h, p, slot], 0, d,
                )

    @pl.when(inner == 1)
    def _():
        for h in range(2):
            for p in range(PARTS):
                nearby[h, p].wait_recv()
                for r in range(rows):
                    at = p * rows + r
                    pieces = split(own[h, at].reshape(2 * back, depth))
                    pieces += split(near[h, at].reshape(2 * back, depth))
                    total = mm(phi_y[...], jnp.concatenate(pieces, axis=0))
                    keep[h, at] = total[4 * out_b : 5 * out_b]
                    for k in range(5):
                        first = (k if k < 4 else 5) * out_b
                        part_out[h, p, k, r] = total[first : first + out_b]
                for k in range(5):
                    parts[h, p, k].start()

    for c in fy:
        c.wait_recv()
    value = fy_out[...]
    for d in range(1, nx):
        value = value + fy_in[d - 1]
    out_y[...] = (value * (1.0 / math.sqrt(front * nx * depth)))[:, :RANK]
    for c in gathered:
        c.wait_recv()
    for c in sm:
        c.wait_send()
    for d in range(ng):
        block = zx_out[...] if d == 0 else zx_in[d - 1]
        small_out[dev_g(d)] = block
    scale_x = 1.0 / math.sqrt(back * ng * depth)
    scale_z = 1.0 / math.sqrt(front * nx * back * ng)
    for d in range(ng):
        out_x[d * per : (d + 1) * per, :] = small_out[d, SUB : SUB + per, :RANK] * scale_x
        out_z[d * kper : (d + 1) * kper, :] = small_out[d, 0:kper] * scale_z

    for c in pend:
        c.wait_send()

    @pl.when(inner == 0)
    def _():
        for c in list(nearby.values()) + list(share.values()):
            c.wait_send()

    @pl.when(inner == 1)
    def _():
        for c in edges.values():
            c.wait_send()

    scale = 1.0 / math.sqrt(front * nx * back * ng * depth)
    count = rows * out_b
    for h in range(2):
        for p in range(PARTS):
            if h or p:
                before = (h, p - 1) if p else (h - 1, PARTS - 1)

                @pl.when(inner == 1)
                def _():
                    for k in range(5):
                        parts[before + (k,)].wait_send()

            @pl.when(inner == 0)
            def _():
                edges[h, p, 0].wait_recv()
                edges[h, p, 1].wait_recv()

            share[h, p, 0].wait_recv()
            parts[h, p, 0].wait_recv()
            parts[h, p, 1].wait_recv()
            at = slice(p * rows, (p + 1) * rows)
            mine = keep[h, at] + part_in[h, p, 3] + part_in[h, p, 1]
            other = part_in[h, p, 0] + part_in[h, p, 4] + part_in[h, p, 2]
            mine = mine.reshape(count, depth)
            other = other.reshape(count, depth)
            high, low = split(jnp.concatenate([mine, other], axis=0))
            value = (mm(high, phi_z[h]) + mm(low, phi_z[h])) * scale
            for i in range(2):
                for which in range(2):
                    side = core if which == 0 else 1 - core
                    start = pl.multiple_of((i * pairs + side * SUB + p * rows) * out_b, SUB)
                    place = pl.ds(start, count)
                    piece = value[which * count : (which + 1) * count, i * LANES : (i + 1) * LANES]
                    out_core[place, :] = piece if h == 0 else out_core[place, :] + piece
    @pl.when(inner == 1)
    def _():
        for k in range(5):
            parts[1, PARTS - 1, k].wait_send()


def publish(*refs):
    ready, out, sems = refs[:4], refs[4:8], refs[8]
    copies = [pltpu.make_async_copy(a, b, sems.at[i]) for i, (a, b) in enumerate(zip(ready, out))]
    for c in copies:
        c.start()
    for c in copies:
        c.wait()


def fused_body(nx, ng, thermal_field, generator_keys, slab_top_offset):
    front, back, depth = thermal_field.shape
    blk_a = TARGET_RANK // nx
    out_b = TARGET_RANK // ng
    f32 = jnp.float32
    bf16 = jnp.bfloat16
    vmem = pltpu.VMEM
    dma = pltpu.SemaphoreType.DMA
    groups = back // SUB
    rows = SUB // PARTS
    scratch = [
        pltpu.SMEM(generator_keys.shape, jnp.int32),
        vmem((front, back, depth), f32),
        dma((2,)),
        vmem((2, groups, front // 2, SUB, depth), f32),
        vmem((2, groups, front // 2, SUB, depth), f32),
        vmem((2, blk_a, back, depth), f32),
        vmem((2, 3, SUB, back, depth), f32),
        vmem((2, SUB, 2, back, depth), f32),
        vmem((2, SUB, 2, back, depth), f32),
        vmem((2, SUB, out_b, depth), f32),
        vmem((2, PARTS, 2, rows, out_b, depth), f32),
        vmem((2, PARTS, 5, rows, out_b, depth), f32),
        vmem((2, PARTS, 5, rows, out_b, depth), f32),
        vmem((2, 2 * blk_a, 2 * front), bf16),
        vmem((2, 2 * blk_a, 2 * front), bf16),
        vmem((6 * out_b, 8 * back), bf16),
        vmem((2 * out_b, 4 * back), bf16),
        vmem((2, depth, 2 * LANES), bf16),
        vmem((ng, 2 * SUB, LANES), f32),
        vmem((ng - 1, 2 * SUB, LANES), f32),
        vmem((2 * SUB, LANES), f32),
        vmem((nx - 1, SUB, LANES), f32),
        vmem((2 * SUB, LANES), f32),
        vmem((ng - 1, 2 * SUB, LANES), f32),
        vmem((back, LANES), f32),
        vmem((nx - 1, back, LANES), f32),
        dma((2, groups)), dma((2, groups)),
        dma((2, PARTS)), dma((2, PARTS)),
        dma((2, PARTS, 2, groups)), dma((2, PARTS, 2, groups)),
        dma((2, PARTS)), dma((2, PARTS)),
        dma((2, PARTS, 5)), dma((2, PARTS, 5)), dma((2, PARTS, 5)),
        dma((nx - 1,)), dma((nx - 1,)),
        dma((ng - 1,)), dma((ng - 1,)),
        dma((nx - 1,)), dma((nx - 1,)),
        dma((ng - 1,)), dma((ng - 1,)),
    ]
    whole = pl.BlockSpec(memory_space=pltpu.VMEM)
    far = pl.BlockSpec(memory_space=pltpu.HBM)
    shapes = (
        jax.ShapeDtypeStruct((front, RANK), f32),
        jax.ShapeDtypeStruct((back, RANK), f32),
        jax.ShapeDtypeStruct((RANK, depth), f32),
        jax.ShapeDtypeStruct((blk_a * out_b, depth), f32),
    )
    def stay(array):
        return pltpu.with_memory_space_constraint(array, pltpu.HBM)

    results = pl.pallas_call(
        functools.partial(kernel, (nx, ng, front, back, depth)),
        out_shape=shapes,
        in_specs=[far, pl.BlockSpec(memory_space=pltpu.SMEM), far],
        out_specs=(whole,) * 4,
        scratch_shapes=scratch,
        compiler_params=pltpu.CompilerParams(
            collective_id=0, has_side_effects=True, vmem_limit_bytes=40 * 2**20
        ),
    )(stay(generator_keys), slab_top_offset, stay(thermal_field))
    fx, fy, fz, core = pl.pallas_call(
        publish,
        out_shape=shapes,
        in_specs=[whole] * 4,
        out_specs=(far,) * 4,
        scratch_shapes=[dma((4,))],
        compiler_params=pltpu.CompilerParams(vmem_limit_bytes=2**20),
    )(*results)
    return fx, fy, fz.T, core.reshape(blk_a, out_b, depth)


def suits(nx, ng):
    return nx == 4 and ng == 8


def solution(mesh):
    nx, ng = mesh.shape["gx"], mesh.shape["gy"]
    chosen = functools.partial(fused_body, nx, ng) if suits(nx, ng) else body
    placed = (P("gx", "gy", None), P(), P())
    return jax.shard_map(
        chosen,
        mesh=mesh,
        in_specs=placed,
        out_specs=(P("gx", None), P("gy", None), P(), P("gx", "gy", None)),
        check_vma=False,
    )
```

```python
import functools
import math

import jax
import jax.numpy as jnp
from jax import lax
from jax.experimental import pallas as pl
from jax.experimental.pallas import tpu as pltpu
from jax.sharding import PartitionSpec as P

RANK = 64
TARGET_RANK = 128


def random_signs(seed_value, cell_index, column_index):
    hashed = cell_index * 73856093 + column_index * 19349663 + seed_value * 83492791
    hashed = jnp.bitwise_xor(hashed, lax.shift_right_logical(hashed, jnp.full_like(hashed, 15)))
    hashed = hashed * 668265261
    hashed = jnp.bitwise_xor(hashed, lax.shift_right_logical(hashed, jnp.full_like(hashed, 13)))
    parity = jnp.bitwise_and(
        lax.shift_right_logical(hashed, jnp.full_like(hashed, 7)), jnp.full_like(hashed, 1)
    )
    return jnp.where(parity == 1, 1.0, -1.0).astype(jnp.float32)


def body(thermal_field, generator_keys, slab_top_offset):
    exact_matmul_mode = lax.Precision.HIGHEST
    front_length, back_length, vertical_layer = thermal_field.shape
    devices_first = lax.axis_size("gx")
    devices_second = lax.axis_size("gy")
    total_first = front_length * devices_first
    total_second = back_length * devices_second
    x_index = (lax.axis_index("gx") * front_length + jnp.arange(front_length, dtype=jnp.int32))[
        :, None
    ]
    y_index = (lax.axis_index("gy") * back_length + jnp.arange(back_length, dtype=jnp.int32))[
        :, None
    ]
    z_index = (slab_top_offset[0] + jnp.arange(vertical_layer, dtype=jnp.int32))[:, None]
    rank_cols = jnp.arange(RANK, dtype=jnp.int32)[None, :]
    core_cols = jnp.arange(TARGET_RANK, dtype=jnp.int32)[None, :]
    omega_x = random_signs(generator_keys[0], x_index, rank_cols)
    omega_y = random_signs(generator_keys[1], y_index, rank_cols)
    omega_z = random_signs(generator_keys[2], z_index, rank_cols)
    phi_xt = random_signs(generator_keys[3], x_index, core_cols).T
    phi_yt = random_signs(generator_keys[4], y_index, core_cols).T
    phi_z = random_signs(generator_keys[5], z_index, core_cols)
    unrolled_grid = thermal_field.reshape(front_length * back_length, vertical_layer)
    reduced = jnp.dot(unrolled_grid, omega_z, precision=exact_matmul_mode).reshape(
        front_length, back_length, RANK
    )
    partial_x = jnp.einsum("xyk,yk->xk", reduced, omega_y, precision=exact_matmul_mode)
    partial_y = jnp.einsum("xyk,xk->yk", reduced, omega_x, precision=exact_matmul_mode)
    khatri = (omega_x[:, None, :] * omega_y[None, :, :]).reshape(front_length * back_length, RANK)
    partial_z = jnp.einsum("pz,pk->zk", unrolled_grid, khatri, precision=exact_matmul_mode)
    summed_x, half_z = lax.psum((partial_x, partial_z), "gy")
    summed_y, summed_z = lax.psum((partial_y, half_z), "gx")
    factor_x = summed_x * (1.0 / math.sqrt(total_second * vertical_layer))
    factor_y = summed_y * (1.0 / math.sqrt(total_first * vertical_layer))
    factor_z = summed_z * (1.0 / math.sqrt(total_first * total_second))
    thermal_matrix = thermal_field.reshape(front_length, back_length * vertical_layer)
    chosen_entries = phi_xt
    reduced_first = lax.psum_scatter(
        jnp.dot(chosen_entries, thermal_matrix, precision=exact_matmul_mode),
        "gx",
        scatter_dimension=0,
        tiled=True,
    )
    reduced_first = reduced_first.reshape(-1, back_length, vertical_layer)
    chosen_entries = phi_yt
    middle = jnp.einsum("by,ayz->baz", chosen_entries, reduced_first, precision=exact_matmul_mode)
    swapped = lax.psum_scatter(
        jnp.einsum("baz,zc->bac", middle, phi_z, precision=exact_matmul_mode),
        "gy",
        scatter_dimension=0,
        tiled=True,
    )
    core_block = jnp.transpose(swapped, (1, 0, 2))
    core = core_block * (1.0 / math.sqrt(total_first * total_second * vertical_layer))
    return (factor_x, factor_y, factor_z, core)


SUB = 8
LANES = 128
PARTS = 2
MESH_ID = pl.DeviceIdType.MESH


def signs(seed_value, cell_index, column_index):
    hashed = cell_index * 73856093 + column_index * 19349663 + seed_value * 83492791
    hashed = hashed ^ lax.shift_right_logical(hashed, jnp.full_like(hashed, 15))
    hashed = hashed * 668265261
    hashed = hashed ^ lax.shift_right_logical(hashed, jnp.full_like(hashed, 13))
    return jnp.where((hashed & 128) != 0, 1.0, -1.0).astype(jnp.float32)


def iota(shape, axis):
    return lax.broadcasted_iota(jnp.int32, shape, axis)


def split(value):
    high = value.astype(jnp.bfloat16)
    low = (value - high.astype(jnp.float32)).astype(jnp.bfloat16)
    return high, low


def mm(left, right):
    return jnp.dot(left, right, preferred_element_type=jnp.float32)


def flip(index, bit):
    return index + bit - 2 * bit * ((index // bit) % 2)


def way_of(group, groups, half):
    if 2 * group + 1 == groups:
        return half
    return 0 if 2 * group < groups else 1


def step_x(ix, way, turn):
    low = flip(ix, 1)
    high = flip(ix, 2)
    first = low + (high - low) * way
    return first if turn == 0 else low + high - first


def kernel(
    dims,
    keys_in, top, field_in,
    out_x, out_y, out_z, out_core,
    keys, field, load_sem, raw_out, raw_in, spread, landed, own, near, keep, edge_out, part_out, part_in,
    first_w, second_w, phi_y, phi_edge, phi_z,
    small_out, small_in, small_sum, zsum_in, zx_out, zx_in, fy_out, fy_in,
    s0, r0, s5, r5, s1, r1, s2, r2, s3, r3, s6, t1, u1, t2, u2, t3, u3, t4, u4,
):
    nx, ng, front, back, depth = dims
    nz = ng // 2
    blk_a = TARGET_RANK // nx
    pairs = blk_a // 2
    out_b = TARGET_RANK // ng
    ix = lax.axis_index("gx")
    ig = lax.axis_index("gy")
    iz, core = ig // 2, ig % 2
    inner = ((iz + 1) // 2) % 2

    def dev_x(d):
        r = ix
        for bit in (1, 2):
            if d & bit:
                r = flip(r, bit)
        return r

    def dev_g(d):
        r = ig
        for bit in (1, 2, 4):
            if d & bit:
                r = flip(r, bit)
        return r

    def copy(src, dst, send, recv, dx, dg):
        return pltpu.make_async_remote_copy(
            src_ref=src, dst_ref=dst, send_sem=send, recv_sem=recv,
            device_id=(dev_x(dx), dev_g(dg)), device_id_type=MESH_ID,
        )

    load = pltpu.make_async_copy(field_in, field, load_sem.at[0])
    load.start()
    load_keys = pltpu.make_async_copy(keys_in, keys, load_sem.at[1])
    load_keys.start()
    partners = [(dx, dc) for dx in range(nx) for dc in range(2) if dx or dc]
    partners += [(0, dg) for dg in range(2, ng)]
    barrier = pltpu.get_barrier_semaphore()
    for dx, dg in partners:
        pl.semaphore_signal(
            barrier, inc=1, device_id=(dev_x(dx), dev_g(dg)), device_id_type=MESH_ID
        )

    x0 = ix * front
    y0 = ig * back
    groups = back // SUB
    order = list(range(0, groups, 2)) + list(range(1, groups, 2))
    fold = front // 2
    deep = depth // 2
    two_d = field.reshape(front * back, depth)
    lower = iota((fold, SUB, depth), 2) < deep
    load.wait()
    for h in range(2):
        for g in order:
            here = field[0:fold, g * SUB : (g + 1) * SUB, :]
            there = field[fold:front, g * SUB : (g + 1) * SUB, :]
            if h == 0:
                raw_out[h, g] = jnp.where(lower, here, pltpu.roll(there, deep, 2))
            else:
                raw_out[h, g] = jnp.where(lower, pltpu.roll(here, deep, 2), there)
    pl.semaphore_wait(barrier, len(partners))
    raws = {}
    for h in range(2):
        for g in order:
            raws[h, g] = pltpu.make_async_remote_copy(
                src_ref=raw_out.at[h, g], dst_ref=raw_in.at[h, g],
                send_sem=s0.at[h, g], recv_sem=r0.at[h, g],
                device_id=(step_x(ix, way_of(g, groups, h), 0), ig), device_id_type=MESH_ID,
            )
            raws[h, g].start()
    pend = list(raws.values())
    load_keys.wait()
    z0 = top[0]

    lane = iota((RANK, 2 * front), 1)
    left = signs(
        keys[0], jnp.where(lane >= front, lane - front, lane) + x0, iota((RANK, 2 * front), 0)
    ).astype(jnp.bfloat16)
    omega_yt = signs(keys[1], iota((RANK, back), 1) + y0, iota((RANK, back), 0))
    total_z = jnp.zeros((RANK, depth), jnp.float32)
    for y in range(back):
        high, low = split(two_d[pl.ds(y, front, stride=back), :])
        both = mm(left, jnp.concatenate([high, low], axis=0))
        total_z = total_z + both * omega_yt[:, y : y + 1]

    lane_z = iota((depth, LANES), 1)
    row_z = iota((depth, LANES), 0) + z0
    omega_z = signs(keys[2], row_z, lane_z).astype(jnp.bfloat16)
    high, low = split(two_d[...])
    reduced = (mm(high, omega_z) + mm(low, omega_z)).reshape(front, back, LANES)
    omega_y = signs(keys[1], iota((back, LANES), 0) + y0, iota((back, LANES), 1))
    part_y = jnp.zeros((back, LANES), jnp.float32)
    omega_x = signs(keys[0], iota((front, LANES), 0) + x0, iota((front, LANES), 1))
    part_x = jnp.sum(reduced * omega_y[None], axis=1)
    for x in range(front):
        part_y = part_y + reduced[x] * omega_x[x : x + 1]
    fy_out[...] = part_y
    per = front // ng
    kper = RANK // ng
    for d in range(ng):
        small_out[d, 0:kper] = total_z[d * kper : (d + 1) * kper]
        small_out[d, SUB : SUB + per] = part_x[d * per : (d + 1) * per]
    sm = []
    for d in range(1, ng):
        sm.append(copy(
            small_out.at[dev_g(d)], small_in.at[d - 1], t2.at[d - 1], u2.at[d - 1], 0, d
        ))
        sm[-1].start()

    def weights(base, far_x):
        shape = (4 * pairs, 4 * fold)
        row = iota(shape, 0)
        lane = iota(shape, 1)
        lane = jnp.where(lane >= front, lane - front, lane)
        second = row >= 2 * pairs
        row = jnp.where(second, row - 2 * pairs, row)
        swapped = jnp.where(lane >= fold, lane - fold, lane + fold)
        cell = jnp.where(second, swapped, lane) + base
        target = jnp.where(row < pairs, ix * blk_a, far_x * blk_a - pairs) + row
        target = jnp.where(second, target + pairs, target)
        return signs(keys[3], cell, target).astype(jnp.bfloat16)

    for way in range(2):
        first_w[way] = weights(x0, step_x(ix, way, 1))
        second_w[way] = weights(step_x(ix, way, 0) * front, step_x(ix, way, 1))

    lower_row = iota((2 * pairs, depth), 1) < deep

    def contract(left, packed):
        both = jnp.concatenate([packed, pltpu.roll(packed, deep, 1)], axis=0)
        high, low = split(both)
        out = mm(left, jnp.concatenate([high, low], axis=0))
        return jnp.where(lower_row, out[: 2 * pairs], out[2 * pairs :])

    for h in range(2):
        wide = spread.at[h].reshape(2 * pairs * back, depth)
        for g in order:
            flat = raw_out.at[h, g].reshape(fold * SUB, depth)
            for y in range(SUB):
                wide[pl.ds(g * SUB + y, 2 * pairs, stride=back), :] = contract(
                    first_w[way_of(g, groups, h)], flat[pl.ds(y, fold, stride=SUB), :]
                )

    shape = (6 * out_b, 4 * back)
    row = iota(shape, 0)
    col = iota(shape, 1)
    col = jnp.where(col >= 2 * back, col - 2 * back, col)
    target = row
    for k, d in enumerate((4, 5, 6, 7, 0, 1)):
        target = jnp.where(row >= k * out_b, row + (dev_g(d) - k) * out_b, target)
    for src in range(2):
        cell = jnp.where(col >= back, dev_g(2 * src + 1) * back - back, dev_g(2 * src) * back) + col
        phi_y[:, src * 4 * back : (src + 1) * 4 * back] = signs(keys[4], cell, target).astype(
            jnp.bfloat16
        )
        if src == 0:
            row = row[: 2 * out_b]
            here = ig + (dev_g(2) - ig) * inner
            there = dev_g(1) + (dev_g(3) - dev_g(1)) * inner
            target_edge = row + jnp.where(row >= out_b, there - 1, here) * out_b
            phi_edge[...] = signs(keys[4], cell[: 2 * out_b], target_edge).astype(jnp.bfloat16)

    @pl.when(inner == 1)
    def _():
        for h in range(2):
            part_in[h, :, 3:5] = jnp.zeros((PARTS, 2, SUB // PARTS, out_b, depth), jnp.float32)

    row = iota((depth, 2 * LANES), 0)
    col = iota((depth, 2 * LANES), 1)
    same = (row >= deep) == (col >= LANES)
    row = jnp.where(row >= deep, row - deep, row) + z0
    col = jnp.where(col >= LANES, col - LANES, col)
    for h in range(2):
        phi_z[h] = jnp.where(same, signs(keys[5], row + h * deep, col), 0.0).astype(jnp.bfloat16)

    rows = SUB // PARTS
    zx = []

    def sum_small():
        for c in sm:
            c.wait_recv()
        block = small_out[ig]
        for d in range(1, ng):
            block = block + small_in[d - 1]
        small_sum[...] = block
        for d in range(1, nx):
            zx.append(copy(
                small_sum.at[0:SUB], zsum_in.at[d - 1], t3.at[d - 1], u3.at[d - 1], d, 0
            ))
            zx[-1].start()

    def receive_raw(h):
        wide = spread.at[h].reshape(2 * pairs * back, depth)
        sends = [[] for _ in range(PARTS)]
        for g in order:
            raws[h, g].wait_recv()
            flat = raw_in.at[h, g].reshape(fold * SUB, depth)
            for y in range(SUB):
                strip = pl.ds(g * SUB + y, 2 * pairs, stride=back)
                wide[strip, :] = wide[strip, :] + contract(
                    second_w[way_of(g, groups, h)], flat[pl.ds(y, fold, stride=SUB), :]
                )
            for p in range(PARTS):
                for dc in (1, 0):
                    start = pairs + (dev_g(dc) % 2) * SUB + p * rows
                    ys = slice(g * SUB, (g + 1) * SUB)
                    sends[p].append(pltpu.make_async_remote_copy(
                        src_ref=spread.at[h, pl.ds(start, rows), ys, :],
                        dst_ref=landed.at[h, dc, p * rows : (p + 1) * rows, ys, :],
                        send_sem=s1.at[h, p, dc, g], recv_sem=r1.at[h, p, dc, g],
                        device_id=(step_x(ix, way_of(g, groups, h), 1), dev_g(dc)),
                        device_id_type=MESH_ID,
                    ))
                    sends[p][-1].start()
        for p in range(PARTS):
            sends[p].append(copy(
                spread.at[h, pl.ds((1 - core) * SUB + p * rows, rows)],
                landed.at[h, 2, p * rows : (p + 1) * rows],
                s5.at[h, p], r5.at[h, p], 0, 1,
            ))
            sends[p][-1].start()
        return sends

    nearby = {}
    edges = {}
    share = {}

    def send_near(h, p, sends):
        for c in sends[p]:
            c.wait_recv()
        at = slice(p * rows, (p + 1) * rows)
        own[h, at, 0] = spread[h, pl.ds(core * SUB + p * rows, rows)] + landed[h, 0, at]
        own[h, at, 1] = landed[h, 2, at] + landed[h, 1, at]
        nearby[h, p] = copy(own.at[h, at], near.at[h, at], s2.at[h, p], r2.at[h, p], 0, 2)

        @pl.when(inner == 0)
        def _():
            nearby[h, p].start()

    def send_edges(h, p):
        at = slice(p * rows, (p + 1) * rows)
        for r in range(rows):
            pieces = split(own[h, p * rows + r].reshape(2 * back, depth))
            total = mm(phi_edge[...], jnp.concatenate(pieces, axis=0))
            edge_out[h, p, 0, r] = total[:out_b]
            edge_out[h, p, 1, r] = total[out_b:]
        for k in range(2):
            edges[h, p, k] = copy(
                edge_out.at[h, p, k], part_in.at[h, p, 3 + k],
                s3.at[h, p, 3 + k], r3.at[h, p, 3 + k], 0, 2 + k,
            )
        share[h, p, 0] = copy(
            edge_out.at[h, p, 1], part_in.at[h, p, 0], s3.at[h, p, 0], r3.at[h, p, 0], 0, 1
        )

        @pl.when(inner == 1)
        def _():
            edges[h, p, 0].start()
            edges[h, p, 1].start()

        @pl.when(inner == 0)
        def _():
            keep[h, at] = edge_out[h, p, 0]
            share[h, p, 0].start()


    first = receive_raw(0)
    sum_small()
    second = receive_raw(1)
    for p in range(PARTS):
        send_near(0, p, first)
    for p in range(PARTS):
        send_edges(0, p)
    for c in zx:
        c.wait_recv()
    zpart = small_sum[0:SUB]
    for d in range(1, nx):
        zpart = zpart + zsum_in[d - 1]
    zx_out[0:SUB] = zpart
    zx_out[SUB:] = small_sum[SUB:]
    gathered = []
    for d in range(1, ng):
        gathered.append(copy(zx_out, zx_in.at[d - 1], t4.at[d - 1], u4.at[d - 1], 0, d))
        gathered[-1].start()
    for p in range(PARTS):
        send_near(1, p, second)
    for p in range(PARTS):
        send_edges(1, p)
    fy = []
    for d in range(1, nx):
        fy.append(copy(fy_out, fy_in.at[d - 1], t1.at[d - 1], u1.at[d - 1], d, 0))
        fy[-1].start()
    pend += fy
    pend += sum(first + second, []) + zx + gathered

    parts = {}
    ways = ((0, 4, 1), (1, 5, 2), (2, 6, 1), (3, 7, 2), (4, 1, 0))
    for h in range(2):
        for p in range(PARTS):
            for k, d, slot in ways:
                parts[h, p, k] = copy(
                    part_out.at[h, p, k], part_in.at[h, p, slot],
                    s6.at[h, p, k], r3.at[h, p, slot], 0, d,
                )

    @pl.when(inner == 1)
    def _():
        for h in range(2):
            for p in range(PARTS):
                nearby[h, p].wait_recv()
                for r in range(rows):
                    at = p * rows + r
                    pieces = split(own[h, at].reshape(2 * back, depth))
                    pieces += split(near[h, at].reshape(2 * back, depth))
                    total = mm(phi_y[...], jnp.concatenate(pieces, axis=0))
                    keep[h, at] = total[4 * out_b : 5 * out_b]
                    for k in range(5):
                        first = (k if k < 4 else 5) * out_b
                        part_out[h, p, k, r] = total[first : first + out_b]
                for k in range(5):
                    parts[h, p, k].start()

    for c in fy:
        c.wait_recv()
    value = fy_out[...]
    for d in range(1, nx):
        value = value + fy_in[d - 1]
    out_y[...] = (value * (1.0 / math.sqrt(front * nx * depth)))[:, :RANK]
    for c in gathered:
        c.wait_recv()
    for c in sm:
        c.wait_send()
    for d in range(ng):
        block = zx_out[...] if d == 0 else zx_in[d - 1]
        small_out[dev_g(d)] = block
    scale_x = 1.0 / math.sqrt(back * ng * depth)
    scale_z = 1.0 / math.sqrt(front * nx * back * ng)
    for d in range(ng):
        out_x[d * per : (d + 1) * per, :] = small_out[d, SUB : SUB + per, :RANK] * scale_x
        out_z[d * kper : (d + 1) * kper, :] = small_out[d, 0:kper] * scale_z

    for c in pend:
        c.wait_send()

    @pl.when(inner == 0)
    def _():
        for c in list(nearby.values()) + list(share.values()):
            c.wait_send()

    @pl.when(inner == 1)
    def _():
        for c in edges.values():
            c.wait_send()

    scale = 1.0 / math.sqrt(front * nx * back * ng * depth)
    count = rows * out_b
    for h in range(2):
        for p in range(PARTS):
            if h or p:
                before = (h, p - 1) if p else (h - 1, PARTS - 1)

                @pl.when(inner == 1)
                def _():
                    for k in range(5):
                        parts[before + (k,)].wait_send()

            @pl.when(inner == 0)
            def _():
                edges[h, p, 0].wait_recv()
                edges[h, p, 1].wait_recv()

            share[h, p, 0].wait_recv()
            parts[h, p, 0].wait_recv()
            parts[h, p, 1].wait_recv()
            at = slice(p * rows, (p + 1) * rows)
            mine = keep[h, at] + part_in[h, p, 3] + part_in[h, p, 1]
            other = part_in[h, p, 0] + part_in[h, p, 4] + part_in[h, p, 2]
            mine = mine.reshape(count, depth)
            other = other.reshape(count, depth)
            high, low = split(jnp.concatenate([mine, other], axis=0))
            value = (mm(high, phi_z[h]) + mm(low, phi_z[h])) * scale
            for i in range(2):
                for which in range(2):
                    side = core if which == 0 else 1 - core
                    start = pl.multiple_of((i * pairs + side * SUB + p * rows) * out_b, SUB)
                    place = pl.ds(start, count)
                    piece = value[which * count : (which + 1) * count, i * LANES : (i + 1) * LANES]
                    out_core[place, :] = piece if h == 0 else out_core[place, :] + piece
    @pl.when(inner == 1)
    def _():
        for k in range(5):
            parts[1, PARTS - 1, k].wait_send()


def publish(*refs):
    ready, out, sems = refs[:4], refs[4:8], refs[8]
    copies = [pltpu.make_async_copy(a, b, sems.at[i]) for i, (a, b) in enumerate(zip(ready, out))]
    for c in copies:
        c.start()
    for c in copies:
        c.wait()


def fused_body(nx, ng, thermal_field, generator_keys, slab_top_offset):
    front, back, depth = thermal_field.shape
    blk_a = TARGET_RANK // nx
    out_b = TARGET_RANK // ng
    f32 = jnp.float32
    bf16 = jnp.bfloat16
    vmem = pltpu.VMEM
    dma = pltpu.SemaphoreType.DMA
    groups = back // SUB
    rows = SUB // PARTS
    scratch = [
        pltpu.SMEM(generator_keys.shape, jnp.int32),
        vmem((front, back, depth), f32),
        dma((2,)),
        vmem((2, groups, front // 2, SUB, depth), f32),
        vmem((2, groups, front // 2, SUB, depth), f32),
        vmem((2, blk_a, back, depth), f32),
        vmem((2, 3, SUB, back, depth), f32),
        vmem((2, SUB, 2, back, depth), f32),
        vmem((2, SUB, 2, back, depth), f32),
        vmem((2, SUB, out_b, depth), f32),
        vmem((2, PARTS, 2, rows, out_b, depth), f32),
        vmem((2, PARTS, 5, rows, out_b, depth), f32),
        vmem((2, PARTS, 5, rows, out_b, depth), f32),
        vmem((2, 2 * blk_a, 2 * front), bf16),
        vmem((2, 2 * blk_a, 2 * front), bf16),
        vmem((6 * out_b, 8 * back), bf16),
        vmem((2 * out_b, 4 * back), bf16),
        vmem((2, depth, 2 * LANES), bf16),
        vmem((ng, 2 * SUB, LANES), f32),
        vmem((ng - 1, 2 * SUB, LANES), f32),
        vmem((2 * SUB, LANES), f32),
        vmem((nx - 1, SUB, LANES), f32),
        vmem((2 * SUB, LANES), f32),
        vmem((ng - 1, 2 * SUB, LANES), f32),
        vmem((back, LANES), f32),
        vmem((nx - 1, back, LANES), f32),
        dma((2, groups)), dma((2, groups)),
        dma((2, PARTS)), dma((2, PARTS)),
        dma((2, PARTS, 2, groups)), dma((2, PARTS, 2, groups)),
        dma((2, PARTS)), dma((2, PARTS)),
        dma((2, PARTS, 5)), dma((2, PARTS, 5)), dma((2, PARTS, 5)),
        dma((nx - 1,)), dma((nx - 1,)),
        dma((ng - 1,)), dma((ng - 1,)),
        dma((nx - 1,)), dma((nx - 1,)),
        dma((ng - 1,)), dma((ng - 1,)),
    ]
    whole = pl.BlockSpec(memory_space=pltpu.VMEM)
    far = pl.BlockSpec(memory_space=pltpu.HBM)
    shapes = (
        jax.ShapeDtypeStruct((front, RANK), f32),
        jax.ShapeDtypeStruct((back, RANK), f32),
        jax.ShapeDtypeStruct((RANK, depth), f32),
        jax.ShapeDtypeStruct((blk_a * out_b, depth), f32),
    )
    def stay(array):
        return pltpu.with_memory_space_constraint(array, pltpu.HBM)

    results = pl.pallas_call(
        functools.partial(kernel, (nx, ng, front, back, depth)),
        out_shape=shapes,
        in_specs=[far, pl.BlockSpec(memory_space=pltpu.SMEM), far],
        out_specs=(whole,) * 4,
        scratch_shapes=scratch,
        compiler_params=pltpu.CompilerParams(
            collective_id=0, has_side_effects=True, vmem_limit_bytes=40 * 2**20
        ),
    )(stay(generator_keys), slab_top_offset, stay(thermal_field))
    fx, fy, fz, core = pl.pallas_call(
        publish,
        out_shape=shapes,
        in_specs=[whole] * 4,
        out_specs=(far,) * 4,
        scratch_shapes=[dma((4,))],
        compiler_params=pltpu.CompilerParams(vmem_limit_bytes=2**20),
    )(*results)
    return fx, fy, fz.T, core.reshape(blk_a, out_b, depth)


def suits(nx, ng):
    return nx == 4 and ng == 8


def solution(mesh):
    nx, ng = mesh.shape["gx"], mesh.shape["gy"]
    chosen = functools.partial(fused_body, nx, ng) if suits(nx, ng) else body
    placed = (P("gx", "gy", None), P(), P())
    return jax.shard_map(
        chosen,
        mesh=mesh,
        in_specs=placed,
        out_specs=(P("gx", None), P("gy", None), P(), P("gx", "gy", None)),
        check_vma=False,
    )
```
